512 devices in a mesh: wide: 64 (over y, z_lo, core), narrow: 8 (over z_hi, x).
Axes of the slice: x: 4, y: 4, z: 16 (z_hi: 2, z_lo: 8; z = z_hi * 8 + z_lo), core: 2. Of those that a mesh axis runs over, the one named last changes fastest.
Arguments:
- voltages: bfloat16 [2, 512, 64, 4096], P(None, 'narrow', 'wide'), may hold values from -6 to 6
- station_flags: int32 [256], replicated, may hold values 0 or 1
- channel_order: int32 [4096], replicated, may hold values from 0 to 4095, each once
- beam_stations: int32 [128, 64], replicated, may hold values from 0 to 255
- beam_weight_re: float32 [128, 64], replicated, may hold values from -0.5 to 0.5
- beam_weight_im: float32 [128, 64], replicated, may hold values from -0.5 to 0.5
Outputs:
- visibilities: float32 [512, 2, 512, 512], P('wide', None, 'narrow')
- beam_power: float32 [4096, 128], P('wide', 'narrow')
The draws below stay inside these ranges and needn't reach their ends.
Inputs may be any that keep to these rules, and one draw needn't show every extreme that they name: `channel_order`: a permutation of the 4096 channel numbers. `beam_stations`: a beam may select a station more than once.
All inputs are finite; a program needn't handle non-finite values.
Results may differ from the reference program's by a relative error of at most 0.0028.
Values may be sent and summed in bfloat16 or wider, within the bound.
No kernel may reach another device: no remote copies, remote signals or barrier semaphores. Data moves between devices by JAX's collectives and lax.ppermute only.
A program may use at most 64 MiB of HBM per device.

```python
import math
import jax
import jax.numpy as jnp
from jax import lax

STATIONS = 256
BEAMS = 128
SEL = 64
TAPS = 8
AVG = 8
CH = 4096
INPUTS = 512
FRAMES = 64


def plant(values, own_key, least, largest):
    index_at = [jax.random.randint(jax.random.fold_in(own_key, axis), (), 0, length) for axis, length in enumerate(values.shape)]
    main_axis = values.shape.index(max(values.shape))
    neighbour = index_at[:main_axis] + [(index_at[main_axis] + 1) % values.shape[main_axis]] + index_at[main_axis + 1:]
    return values.at[tuple(index_at)].set(least).at[tuple(neighbour)].set(largest)


def level_of(stream_key, extent, pieces, smallest, high):
    def one(dim, parts):
        draws = jax.random.uniform(jax.random.fold_in(jax.random.fold_in(stream_key, 6), dim), (parts,), jnp.float32, smallest / len(pieces), high / len(pieces))
        return jnp.repeat(jnp.exp(draws), extent[dim] // parts).reshape((-1,) + (1,) * (len(extent) - dim - 1))

    loudness = one(*pieces[0])
    for cut in pieces[1:]:
        loudness = loudness * one(*cut)
    return loudness


def centred(key, extent, width, limit, pieces=(), held_as=jnp.bfloat16):
    result = width * jax.random.normal(key, extent, jnp.float32)
    if pieces:
        result = result * level_of(key, extent, pieces, -0.22, 0.18)
    return jnp.clip(result, -limit, limit).astype(held_as)


def setup_inputs(seed: int = 0) -> dict:
    splits = jax.random.split(jax.random.key(seed), 7)
    return {
        "voltages": centred(splits[0], (2, INPUTS, FRAMES, CH), 1.0, 6.0, ((1, 8), (2, 64))),
        "station_flags": plant((jax.random.randint(splits[1], (STATIONS,), 0, 8) < 7).astype(jnp.int32), jax.random.fold_in(splits[1], 1), 0, 1),
        "channel_order": jax.random.permutation(splits[2], CH).astype(jnp.int32),
        "beam_stations": plant(jax.random.randint(splits[3], (BEAMS, SEL), 0, STATIONS), jax.random.fold_in(splits[3], 1), 0, STATIONS - 1).astype(jnp.int32),
        "beam_weight_re": centred(splits[4], (BEAMS, SEL), (2 * SEL) ** -0.5, 0.5, (), jnp.float32),
        "beam_weight_im": centred(splits[5], (BEAMS, SEL), (2 * SEL) ** -0.5, 0.5, (), jnp.float32),
    }


def prototype(tap_count, length):
    places = jnp.arange(tap_count * length, dtype=jnp.float32)
    offsets = places / length - tap_count / 2.0
    window = 0.5 - 0.5 * jnp.cos(2.0 * jnp.pi * (places + 0.5) / (tap_count * length))
    return (jnp.sinc(offsets) * window).reshape(tap_count, length)

def dense_weights(selection, weight_re, weight_im, station_count):
    beam_count, pick_count = selection.shape
    beam_rows = lax.broadcasted_iota(jnp.int32, (beam_count, pick_count), 0)
    flat_index = (beam_rows * station_count + selection).reshape(-1).astype(jnp.int32)
    summed_re = jax.ops.segment_sum(weight_re.reshape(-1), flat_index, num_segments=beam_count * station_count)
    summed_im = jax.ops.segment_sum(weight_im.reshape(-1), flat_index, num_segments=beam_count * station_count)
    return (summed_re.reshape(beam_count, station_count).astype(jnp.bfloat16), summed_im.reshape(beam_count, station_count).astype(jnp.bfloat16))

def filter_block(volt_block, coefficients, channel_order, input_gain):
    frame_count = volt_block.shape[2]
    tap_count = coefficients.shape[0]
    padded = jnp.pad(volt_block.astype(jnp.float32), ((0, 0), (0, 0), (tap_count - 1, 0), (0, 0)))
    filtered = jnp.zeros(volt_block.shape, jnp.float32)
    for tap_index in range(tap_count):
        begin = tap_count - 1 - tap_index
        filtered = filtered + coefficients[tap_index] * padded[:, :, begin:begin + frame_count, :]
    spectrum = jnp.fft.fft(filtered[0] + 1j * filtered[1], axis=-1) / math.sqrt(volt_block.shape[3])
    chosen = jnp.take(spectrum, channel_order, axis=-1)
    gain_view = input_gain[:, None, None]
    part_re = (jnp.real(chosen) * gain_view).astype(jnp.bfloat16)
    part_im = (jnp.imag(chosen) * gain_view).astype(jnp.bfloat16)
    return jnp.stack([part_re, part_im], axis=0)

def reference(voltages, station_flags, channel_order, beam_stations, beam_weight_re, beam_weight_im):
    input_count = voltages.shape[1]
    frame_count = voltages.shape[2]
    length = voltages.shape[3]
    coefficients = prototype(TAPS, length)
    input_gain = jnp.repeat(station_flags, 2).astype(jnp.float32)
    block_count = math.gcd(input_count, 16)
    block_size = input_count // block_count
    volt_blocks = voltages.reshape(2, block_count, block_size, frame_count, length).transpose(1, 0, 2, 3, 4)
    gain_blocks = input_gain.reshape(block_count, block_size)

    def channelize(entry_pair):
        return filter_block(entry_pair[0], coefficients, channel_order, entry_pair[1])
    spectra = lax.map(channelize, (volt_blocks, gain_blocks))
    spectra = spectra.transpose(1, 0, 2, 3, 4).reshape(2, input_count, frame_count, length)
    group_count = length // AVG
    grouped = spectra.reshape(2, input_count, frame_count, group_count, AVG).transpose(3, 0, 1, 2, 4)
    matrix_re, matrix_im = dense_weights(beam_stations, beam_weight_re, beam_weight_im, input_count // 2)
    vis_scale = 1.0 / math.sqrt(AVG * frame_count)

    def correlate(group_entry):
        rows_re = group_entry[0].reshape(input_count, frame_count * AVG)
        rows_im = group_entry[1].reshape(input_count, frame_count * AVG)
        vis_re = jnp.dot(rows_re, rows_re.T, preferred_element_type=jnp.float32) + jnp.dot(rows_im, rows_im.T, preferred_element_type=jnp.float32)
        vis_im = jnp.dot(rows_im, rows_re.T, preferred_element_type=jnp.float32) - jnp.dot(rows_re, rows_im.T, preferred_element_type=jnp.float32)
        vis_pair = jnp.stack([vis_re, vis_im], axis=0) * vis_scale
        station_re = group_entry[0].reshape(input_count // 2, 2 * frame_count * AVG)
        station_im = group_entry[1].reshape(input_count // 2, 2 * frame_count * AVG)
        beam_re = jnp.dot(matrix_re, station_re, preferred_element_type=jnp.float32) - jnp.dot(matrix_im, station_im, preferred_element_type=jnp.float32)
        beam_im = jnp.dot(matrix_re, station_im, preferred_element_type=jnp.float32) + jnp.dot(matrix_im, station_re, preferred_element_type=jnp.float32)
        energy = (beam_re * beam_re + beam_im * beam_im).reshape(-1, 2, frame_count, AVG)
        energy = lax.optimization_barrier(jnp.sum(energy, axis=(1, 2))) / frame_count
        return (vis_pair, energy)
    visibilities, energies = lax.map(correlate, grouped)
    beam_power = energies.transpose(0, 2, 1).reshape(length, -1)
    return (visibilities, beam_power)
```

```python
import math

import jax
import jax.numpy as jnp
import numpy as np
from jax import lax
from jax.experimental import pallas as pl
from jax.experimental.pallas import tpu as pltpu
from jax.sharding import PartitionSpec as P

TAPS = 8
AVG = 8
LANES = 128
OUTER = 32
ROWS = 16


def prototype(tap_count, length):
    places = jnp.arange(tap_count * length, dtype=jnp.float32)
    offsets = places / length - tap_count / 2.0
    window = 0.5 - 0.5 * jnp.cos(2.0 * jnp.pi * (places + 0.5) / (tap_count * length))
    return (jnp.sinc(offsets) * window).reshape(tap_count, length)


def fourier_tables():
    length = OUTER * LANES
    inner = np.arange(LANES, dtype=np.float64)
    angle = 2.0 * np.pi * np.arange(OUTER, dtype=np.float64)[:, None] * inner[None, :] / length
    twist = np.stack([np.cos(angle), -np.sin(angle)]).astype(np.float32)
    turn = 2.0 * np.pi * ((np.arange(LANES)[:, None] * np.arange(LANES)[None, :]) % LANES) / LANES
    cos, sin = np.cos(turn), np.sin(turn)
    matrix = (np.block([[cos, -sin], [sin, cos]]) / math.sqrt(length)).astype(np.float32)
    high = matrix.astype(jnp.bfloat16)
    low = (matrix - high.astype(np.float32)).astype(jnp.bfloat16)
    return twist, high, low


def add(a, b):
    return (a[0] + b[0], a[1] + b[1])


def sub(a, b):
    return (a[0] - b[0], a[1] - b[1])


def turned(a, num, den):
    num %= den
    if num == 0:
        return a
    if 4 * num == den:
        return (a[1], -a[0])
    if 2 * num == den:
        return (-a[0], -a[1])
    if 4 * num == 3 * den:
        return (-a[1], a[0])
    cos, sin = math.cos(2.0 * math.pi * num / den), math.sin(2.0 * math.pi * num / den)
    return (a[0] * cos + a[1] * sin, a[1] * cos - a[0] * sin)


def four(x):
    s0, s1, s2, s3 = add(x[0], x[2]), sub(x[0], x[2]), add(x[1], x[3]), sub(x[1], x[3])
    r3 = turned(s3, 1, 4)
    return [add(s0, s2), add(s1, r3), sub(s0, s2), sub(s1, r3)]


def eight(x):
    even, odd = four(x[0::2]), four(x[1::2])
    odd = [turned(odd[q], q, 8) for q in range(4)]
    return [add(even[q], odd[q]) for q in range(4)] + [sub(even[q], odd[q]) for q in range(4)]


def channelize_kernel(index, *refs):
    frames_re, frames_im = refs[:TAPS], refs[TAPS : 2 * TAPS]
    coeffs, twist, high, low, gain, out, mid, y_hi, y_lo, spec, lined, picked = refs[2 * TAPS :]
    step = pl.program_id(0)

    def filtered(frames, block):
        span = slice(block * LANES, (block + 1) * LANES)
        total = coeffs[0:1, span] * frames[0][:, span].astype(jnp.float32)
        for tap in range(1, TAPS):
            total = total + coeffs[tap : tap + 1, span] * frames[tap][:, span].astype(jnp.float32)
        return total

    for j in range(8):
        points = [
            (filtered(frames_re, j + 8 * m), filtered(frames_im, j + 8 * m)) for m in range(4)
        ]
        for p, value in enumerate(four(points)):
            value = turned(value, j * p, OUTER)
            mid[p, j, 0] = value[0]
            mid[p, j, 1] = value[1]
    for p in range(4):
        for q, value in enumerate(eight([(mid[p, j, 0], mid[p, j, 1]) for j in range(8)])):
            c = p + 4 * q
            cos, sin = twist[0, c : c + 1, :], twist[1, c : c + 1, :]
            rows = slice(c * ROWS, (c + 1) * ROWS)
            for part, y in enumerate(
                (value[0] * cos - value[1] * sin, value[0] * sin + value[1] * cos)
            ):
                upper = y.astype(jnp.bfloat16)
                lanes = slice(part * LANES, (part + 1) * LANES)
                y_hi[rows, lanes] = upper
                y_lo[rows, lanes] = (y - upper.astype(jnp.float32)).astype(jnp.bfloat16)

    def dot(a, b):
        return jnp.dot(a[...], b[...], preferred_element_type=jnp.float32)

    result = dot(y_hi, high) + (dot(y_lo, high) + dot(y_hi, low))
    start = pl.multiple_of(step * ROWS, ROWS)
    for part in range(2):
        spec[:, part, pl.ds(start, ROWS), :] = result[:, part * LANES : (part + 1) * LANES].reshape(
            OUTER, ROWS, LANES
        )

    @pl.when(step == pl.num_programs(0) - 1)
    def _():
        width = spec.shape[2]

        def line(c, carry):
            block = spec[c].reshape(2 * width, LANES)
            lined[pl.ds(pl.multiple_of(c * LANES, LANES), LANES), :] = block.T * gain[...]
            return carry

        lax.fori_loop(0, OUTER, line, 0)
        batch = 16

        def pick(g, carry):
            base = pl.multiple_of(g * batch, batch)
            for j in range(batch):
                picked[pl.ds(base + j, 1), :] = lined[pl.ds(index[base + j], 1), :]
            return carry

        lax.fori_loop(0, OUTER * LANES // batch, pick, 0)
        out[...] = picked[...].reshape(out.shape).astype(jnp.bfloat16)


def channelize(frames_re, frames_im, coeffs, index, gain):
    width, length = frames_re[0].shape
    twist, high, low = fourier_tables()
    frame = pl.BlockSpec((ROWS, length), lambda i, idx: (i, 0))

    def whole(shape):
        return pl.BlockSpec(shape, lambda i, idx: (0,) * len(shape))

    return pl.pallas_call(
        channelize_kernel,
        out_shape=jax.ShapeDtypeStruct((length // AVG, AVG, 2 * width), jnp.bfloat16),
        grid_spec=pltpu.PrefetchScalarGridSpec(
            num_scalar_prefetch=1,
            grid=(width // ROWS,),
            in_specs=[frame] * (2 * TAPS)
            + [whole(coeffs.shape), whole(twist.shape), whole(high.shape), whole(low.shape)]
            + [whole(gain.shape)],
            out_specs=whole((length // AVG, AVG, 2 * width)),
            scratch_shapes=[
                pltpu.VMEM((4, 8, 2, ROWS, LANES), jnp.float32),
                pltpu.VMEM((OUTER * ROWS, 2 * LANES), jnp.bfloat16),
                pltpu.VMEM((OUTER * ROWS, 2 * LANES), jnp.bfloat16),
                pltpu.VMEM((OUTER, 2, width, LANES), jnp.float32),
                pltpu.VMEM((length, 2 * width), jnp.float32),
                pltpu.VMEM((length, 2 * width), jnp.float32),
            ],
        ),
        compiler_params=pltpu.CompilerParams(dimension_semantics=("arbitrary",)),
        name="channelize",
    )(index, *frames_re, *frames_im, coeffs, jnp.asarray(twist), jnp.asarray(high), jnp.asarray(low), gain)


def weights_kernel(stations, weight_re, weight_im, out):
    inputs = out.shape[0] // 2
    beams = stations.shape[1]
    chunk = 64

    def block(n, carry):
        start = pl.multiple_of(n * chunk, chunk)
        rows = lax.broadcasted_iota(jnp.int32, (chunk, beams), 0) + start
        station = rows // 2

        def pick(t, sums):
            here = stations[pl.ds(t, 1), :] == station
            return (
                sums[0] + jnp.where(here, weight_re[pl.ds(t, 1), :], 0.0),
                sums[1] + jnp.where(here, weight_im[pl.ds(t, 1), :], 0.0),
            )

        zero = jnp.zeros((chunk, beams), jnp.float32)
        sum_re, sum_im = lax.fori_loop(0, stations.shape[0], pick, (zero, zero), unroll=4)
        for pol in range(2):
            own = rows % 2 == pol
            part_re = jnp.where(own, sum_re, 0.0).astype(jnp.bfloat16)
            part_im = jnp.where(own, sum_im, 0.0).astype(jnp.bfloat16)
            first = slice(2 * pol * beams, (2 * pol + 1) * beams)
            second = slice((2 * pol + 1) * beams, (2 * pol + 2) * beams)
            out[pl.ds(start, chunk), first] = part_re
            out[pl.ds(start, chunk), second] = part_im
            out[pl.ds(inputs + start, chunk), first] = -part_im
            out[pl.ds(inputs + start, chunk), second] = part_re
        return carry

    lax.fori_loop(0, inputs // chunk, block, 0)


def beam_weights(beam_stations, weight_re, weight_im, input_count):
    beams = beam_stations.shape[0]
    return pl.pallas_call(
        weights_kernel,
        out_shape=jax.ShapeDtypeStruct((2 * input_count, 4 * beams), jnp.bfloat16),
        name="beam_weights",
    )(beam_stations.T, weight_re.T, weight_im.T)


def correlate_kernel(voices, weights, out, x_ref, xt_ref):
    frames, groups, avg, width = voices.shape
    half = width // 2
    count = groups * half
    depth = frames * avg
    lane = lax.broadcasted_iota(jnp.int32, (depth, width), 1)
    for m in range(groups // 2):
        a = voices[:, 2 * m].astype(jnp.float32).reshape(depth, width)
        b = voices[:, 2 * m + 1].astype(jnp.float32).reshape(depth, width)
        re = jnp.where(lane < half, a, pltpu.roll(b, half, 1))
        im = jnp.where(lane < half, pltpu.roll(a, half, 1), b)
        for part, value in enumerate((re, im)):
            span = slice(part * count + m * width, part * count + (m + 1) * width)
            x_ref[:, span] = value.astype(jnp.bfloat16)
            xt_ref[span, :] = value.T.astype(jnp.bfloat16)

    def dot(a, b):
        return jnp.dot(a, b, preferred_element_type=jnp.float32)

    power = dot(x_ref[...], weights[...])
    power = power * power
    beams = power.shape[1] // 4
    energy = power[:, :beams] + power[:, beams : 2 * beams]
    energy = energy + (power[:, 2 * beams : 3 * beams] + power[:, 3 * beams :])
    energy = jnp.sum(energy.reshape(frames, avg, beams), axis=0) / frames
    first = energy.astype(jnp.bfloat16)
    rest = energy - first.astype(jnp.float32)
    second = rest.astype(jnp.bfloat16)
    third = (rest - second.astype(jnp.float32)).astype(jnp.bfloat16)
    terms = jnp.concatenate([first, second, third, jnp.zeros_like(first)], axis=1)

    scale = 1.0 / math.sqrt(depth)
    x_re, x_im = x_ref[:, :count], x_ref[:, count:]
    for r in range(groups):
        xt_re = xt_ref[r * half : (r + 1) * half, :]
        xt_im = xt_ref[count + r * half : count + (r + 1) * half, :]
        out[r, :half, :] = ((dot(xt_re, x_re) + dot(xt_im, x_im)) * scale).astype(jnp.bfloat16)
        out[r, half:width, :] = ((dot(xt_im, x_re) - dot(xt_re, x_im)) * scale).astype(jnp.bfloat16)
        out[r, width:, :] = terms


def correlate(voices, weights):
    frames, groups, avg, width = voices.shape
    count = groups * width // 2
    depth = frames * avg
    return pl.pallas_call(
        correlate_kernel,
        out_shape=jax.ShapeDtypeStruct((groups, width + avg, count), jnp.bfloat16),
        scratch_shapes=[
            pltpu.VMEM((depth, 2 * count), jnp.bfloat16),
            pltpu.VMEM((2 * count, depth), jnp.bfloat16),
        ],
        name="correlate",
    )(voices, weights)


def shards(voltages, station_flags, channel_order, beam_stations, beam_weight_re, beam_weight_im):
    _, width, _, length = voltages.shape
    wide, narrow = lax.axis_size("wide"), lax.axis_size("narrow")
    coeffs = prototype(TAPS, length)
    following = [(d, d + 1) for d in range(wide - 1)]
    streams = []
    own = [voltages[part, :, 0, :] for part in range(2)]
    streams = [[own[0]], [own[1]]]
    for _ in range(TAPS - 1):
        for stream in streams:
            stream.append(lax.ppermute(stream[-1], "wide", following))

    own_flags = lax.dynamic_slice_in_dim(
        station_flags, lax.axis_index("narrow") * (width // 2), width // 2
    )
    gain = jnp.tile(jnp.repeat(own_flags, 2).astype(jnp.float32), 2)[None, :]
    index = channel_order % OUTER * LANES + channel_order // OUTER
    spectra = channelize(streams[0], streams[1], coeffs, index, gain)
    turned_over = lax.all_to_all(spectra, ("wide", "narrow"), 0, 0, tiled=True)
    voices = turned_over.reshape(wide, narrow, AVG, 2 * width)
    weights = beam_weights(beam_stations, beam_weight_re, beam_weight_im, width * narrow)
    sent = correlate(voices, weights)
    back = lax.all_to_all(sent, "narrow", 0, 0, tiled=True)
    visibilities = back[:, : 2 * width].astype(jnp.float32).reshape(narrow, 2, width, -1)
    beams = beam_stations.shape[0]
    terms = back[:, 2 * width :].astype(jnp.float32).reshape(narrow * AVG, -1)
    energy = terms[:, :beams] + terms[:, beams : 2 * beams] + terms[:, 2 * beams : 3 * beams]
    share = beams // narrow
    beam_power = lax.dynamic_slice_in_dim(energy, lax.axis_index("narrow") * share, share, axis=1)
    return (visibilities, beam_power)


def solution(mesh):
    return jax.shard_map(
        shards,
        mesh=mesh,
        in_specs=(P(None, "narrow", "wide", None), P(), P(), P(), P(), P()),
        out_specs=(P("wide", None, "narrow", None), P("wide", "narrow")),
        check_vma=False,
    )
```

```python
import math

import jax
import jax.numpy as jnp
import numpy as np
from jax import lax
from jax.experimental import pallas as pl
from jax.experimental.pallas import tpu as pltpu
from jax.sharding import PartitionSpec as P

TAPS = 8
AVG = 8
LANES = 128
OUTER = 32
ROWS = 16


LEAD = 4
TAPS_FIRST = (4, 2, 6, 0, 3, 1, 5, 7, TAPS)
TAPS_SECOND = (4, 2, 6, 0, 5, 3, 7, TAPS, 1)
HELD = len(TAPS_FIRST)


def prototype(tap_count, length):
    places = jnp.arange(tap_count * length, dtype=jnp.float32)
    offsets = places / length - tap_count / 2.0
    window = 0.5 - 0.5 * jnp.cos(2.0 * jnp.pi * (places + 0.5) / (tap_count * length))
    return (jnp.sinc(offsets) * window).reshape(tap_count, length)


def fourier_tables():
    length = OUTER * LANES
    inner = np.arange(LANES, dtype=np.float64)
    angle = 2.0 * np.pi * np.arange(OUTER, dtype=np.float64)[:, None] * inner[None, :] / length
    twist = np.stack([np.cos(angle), -np.sin(angle)]).astype(np.float32)
    turn = 2.0 * np.pi * ((np.arange(LANES)[:, None] * np.arange(LANES)[None, :]) % LANES) / LANES
    cos, sin = np.cos(turn), np.sin(turn)
    matrix = (np.block([[cos, -sin], [sin, cos]]) / math.sqrt(length)).astype(np.float32)
    high = matrix.astype(jnp.bfloat16)
    low = (matrix - high.astype(np.float32)).astype(jnp.bfloat16)
    return twist, high, low


def add(a, b):
    return (a[0] + b[0], a[1] + b[1])


def sub(a, b):
    return (a[0] - b[0], a[1] - b[1])


def turned(a, num, den):
    num %= den
    if num == 0:
        return a
    if 4 * num == den:
        return (a[1], -a[0])
    if 2 * num == den:
        return (-a[0], -a[1])
    if 4 * num == 3 * den:
        return (-a[1], a[0])
    cos, sin = math.cos(2.0 * math.pi * num / den), math.sin(2.0 * math.pi * num / den)
    return (a[0] * cos + a[1] * sin, a[1] * cos - a[0] * sin)


def four(x):
    s0, s1, s2, s3 = add(x[0], x[2]), sub(x[0], x[2]), add(x[1], x[3]), sub(x[1], x[3])
    r3 = turned(s3, 1, 4)
    return [add(s0, s2), add(s1, r3), sub(s0, s2), sub(s1, r3)]


def eight(x):
    even, odd = four(x[0::2]), four(x[1::2])
    odd = [turned(odd[q], q, 8) for q in range(4)]
    return [add(even[q], odd[q]) for q in range(4)] + [sub(even[q], odd[q]) for q in range(4)]


def channelize_kernel(index, *refs):
    frames_re, frames_im = refs[:HELD], refs[HELD : 2 * HELD]
    coeffs, twist, high, low, gain, out, mid, y_hi, y_lo, spec, lined, picked = refs[2 * HELD :]
    step = pl.program_id(0)

    def filtered(frames, block):
        span = slice(block * LANES, (block + 1) * LANES)
        total = coeffs[0:1, span] * frames[0][:, span].astype(jnp.float32)
        for tap in range(1, HELD):
            total = total + coeffs[tap : tap + 1, span] * frames[tap][:, span].astype(jnp.float32)
        return total

    for j in range(8):
        points = [
            (filtered(frames_re, j + 8 * m), filtered(frames_im, j + 8 * m)) for m in range(4)
        ]
        for p, value in enumerate(four(points)):
            value = turned(value, j * p, OUTER)
            mid[p, j, 0] = value[0]
            mid[p, j, 1] = value[1]
    for p in range(4):
        for q, value in enumerate(eight([(mid[p, j, 0], mid[p, j, 1]) for j in range(8)])):
            c = p + 4 * q
            cos, sin = twist[0, c : c + 1, :], twist[1, c : c + 1, :]
            rows = slice(c * ROWS, (c + 1) * ROWS)
            for part, y in enumerate(
                (value[0] * cos - value[1] * sin, value[0] * sin + value[1] * cos)
            ):
                upper = y.astype(jnp.bfloat16)
                lanes = slice(part * LANES, (part + 1) * LANES)
                y_hi[rows, lanes] = upper
                y_lo[rows, lanes] = (y - upper.astype(jnp.float32)).astype(jnp.bfloat16)

    def dot(a, b):
        return jnp.dot(a[...], b[...], preferred_element_type=jnp.float32)

    result = dot(y_hi, high) + (dot(y_lo, high) + dot(y_hi, low))
    start = pl.multiple_of(step * ROWS, ROWS)
    for part in range(2):
        spec[:, part, pl.ds(start, ROWS), :] = result[:, part * LANES : (part + 1) * LANES].reshape(
            OUTER, ROWS, LANES
        )

    @pl.when(step == pl.num_programs(0) - 1)
    def _():
        width = spec.shape[2]

        def line(c, carry):
            block = spec[c].reshape(2 * width, LANES)
            lined[pl.ds(pl.multiple_of(c * LANES, LANES), LANES), :] = block.T * gain[...]
            return carry

        lax.fori_loop(0, OUTER, line, 0)
        batch = 16

        def pick(g, carry):
            base = pl.multiple_of(g * batch, batch)
            for j in range(batch):
                picked[pl.ds(base + j, 1), :] = lined[pl.ds(index[base + j], 1), :]
            return carry

        lax.fori_loop(0, OUTER * LANES // batch, pick, 0)
        out[...] = picked[...].reshape(out.shape).astype(jnp.bfloat16)


def channelize(frames_re, frames_im, coeffs, index, gain):
    width, length = frames_re[0].shape
    twist, high, low = fourier_tables()
    frame = pl.BlockSpec((ROWS, length), lambda i, idx: (i, 0))

    def whole(shape):
        return pl.BlockSpec(shape, lambda i, idx: (0,) * len(shape))

    return pl.pallas_call(
        channelize_kernel,
        out_shape=jax.ShapeDtypeStruct((length // AVG, AVG, 2 * width), jnp.bfloat16),
        grid_spec=pltpu.PrefetchScalarGridSpec(
            num_scalar_prefetch=1,
            grid=(width // ROWS,),
            in_specs=[frame] * (2 * HELD)
            + [whole(coeffs.shape), whole(twist.shape), whole(high.shape), whole(low.shape)]
            + [whole(gain.shape)],
            out_specs=whole((length // AVG, AVG, 2 * width)),
            scratch_shapes=[
                pltpu.VMEM((4, 8, 2, ROWS, LANES), jnp.float32),
                pltpu.VMEM((OUTER * ROWS, 2 * LANES), jnp.bfloat16),
                pltpu.VMEM((OUTER * ROWS, 2 * LANES), jnp.bfloat16),
                pltpu.VMEM((OUTER, 2, width, LANES), jnp.float32),
                pltpu.VMEM((length, 2 * width), jnp.float32),
                pltpu.VMEM((length, 2 * width), jnp.float32),
            ],
        ),
        compiler_params=pltpu.CompilerParams(dimension_semantics=("arbitrary",)),
        name="channelize",
    )(index, *frames_re, *frames_im, coeffs, jnp.asarray(twist), jnp.asarray(high), jnp.asarray(low), gain)


def weights_kernel(stations, weight_re, weight_im, out):
    inputs = out.shape[0] // 2
    beams = stations.shape[1]
    chunk = 64

    def block(n, carry):
        start = pl.multiple_of(n * chunk, chunk)
        rows = lax.broadcasted_iota(jnp.int32, (chunk, beams), 0) + start
        station = rows // 2

        def pick(t, sums):
            here = stations[pl.ds(t, 1), :] == station
            return (
                sums[0] + jnp.where(here, weight_re[pl.ds(t, 1), :], 0.0),
                sums[1] + jnp.where(here, weight_im[pl.ds(t, 1), :], 0.0),
            )

        zero = jnp.zeros((chunk, beams), jnp.float32)
        sum_re, sum_im = lax.fori_loop(0, stations.shape[0], pick, (zero, zero), unroll=4)
        for pol in range(2):
            own = rows % 2 == pol
            part_re = jnp.where(own, sum_re, 0.0).astype(jnp.bfloat16)
            part_im = jnp.where(own, sum_im, 0.0).astype(jnp.bfloat16)
            first = slice(2 * pol * beams, (2 * pol + 1) * beams)
            second = slice((2 * pol + 1) * beams, (2 * pol + 2) * beams)
            out[pl.ds(start, chunk), first] = part_re
            out[pl.ds(start, chunk), second] = part_im
            out[pl.ds(inputs + start, chunk), first] = -part_im
            out[pl.ds(inputs + start, chunk), second] = part_re
        return carry

    lax.fori_loop(0, inputs // chunk, block, 0)


def beam_weights(beam_stations, weight_re, weight_im, input_count):
    beams = beam_stations.shape[0]
    return pl.pallas_call(
        weights_kernel,
        out_shape=jax.ShapeDtypeStruct((2 * input_count, 4 * beams), jnp.bfloat16),
        name="beam_weights",
    )(beam_stations.T, weight_re.T, weight_im.T)


def correlate_kernel(voices, weights, out, x_ref, xt_ref):
    frames, groups, avg, width = voices.shape
    half = width // 2
    count = groups * half
    depth = frames * avg
    lane = lax.broadcasted_iota(jnp.int32, (depth, width), 1)
    for m in range(groups // 2):
        a = voices[:, 2 * m].astype(jnp.float32).reshape(depth, width)
        b = voices[:, 2 * m + 1].astype(jnp.float32).reshape(depth, width)
        re = jnp.where(lane < half, a, pltpu.roll(b, half, 1))
        im = jnp.where(lane < half, pltpu.roll(a, half, 1), b)
        for part, value in enumerate((re, im)):
            span = slice(part * count + m * width, part * count + (m + 1) * width)
            x_ref[:, span] = value.astype(jnp.bfloat16)
            xt_ref[span, :] = value.T.astype(jnp.bfloat16)

    def dot(a, b):
        return jnp.dot(a, b, preferred_element_type=jnp.float32)

    power = dot(x_ref[...], weights[...])
    power = power * power
    beams = power.shape[1] // 4
    energy = power[:, :beams] + power[:, beams : 2 * beams]
    energy = energy + (power[:, 2 * beams : 3 * beams] + power[:, 3 * beams :])
    energy = jnp.sum(energy.reshape(frames, avg, beams), axis=0) / frames
    first = energy.astype(jnp.bfloat16)
    rest = energy - first.astype(jnp.float32)
    second = rest.astype(jnp.bfloat16)
    third = (rest - second.astype(jnp.float32)).astype(jnp.bfloat16)
    terms = jnp.concatenate([first, second, third, jnp.zeros_like(first)], axis=1)

    scale = 1.0 / math.sqrt(depth)
    x_re, x_im = x_ref[:, :count], x_ref[:, count:]
    for r in range(groups):
        xt_re = xt_ref[r * half : (r + 1) * half, :]
        xt_im = xt_ref[count + r * half : count + (r + 1) * half, :]
        out[r, :half, :] = ((dot(xt_re, x_re) + dot(xt_im, x_im)) * scale).astype(jnp.bfloat16)
        out[r, half:width, :] = ((dot(xt_im, x_re) - dot(xt_re, x_im)) * scale).astype(jnp.bfloat16)
        out[r, width:, :] = terms


def correlate(voices, weights):
    frames, groups, avg, width = voices.shape
    count = groups * width // 2
    depth = frames * avg
    return pl.pallas_call(
        correlate_kernel,
        out_shape=jax.ShapeDtypeStruct((groups, width + avg, count), jnp.bfloat16),
        scratch_shapes=[
            pltpu.VMEM((depth, 2 * count), jnp.bfloat16),
            pltpu.VMEM((2 * count, depth), jnp.bfloat16),
        ],
        name="correlate",
    )(voices, weights)


def held_coefficients(length, wide):
    place = lax.axis_index("wide")
    frame = (place + LEAD) % wide
    taps = jnp.where(place % 2 == 0, jnp.array(TAPS_FIRST), jnp.array(TAPS_SECOND))
    picked = taps[:, None] == jnp.arange(TAPS)[None, :]
    used = jnp.logical_and(picked, (taps <= frame)[:, None])
    table = prototype(TAPS, length)
    rows = [jnp.where(used[:, tap, None], table[tap], 0.0) for tap in range(TAPS)]
    return sum(rows[1:], rows[0])


def gather_frames(own, coeffs, wide):
    def send(value, step, places):
        return lax.ppermute(value, "wide", [(d, (d + step) % wide) for d in places])

    every, first, second = range(wide), range(0, wide, 2), range(1, wide, 2)

    def swap(value):
        pairs = [(d, d ^ 1) for d in every]
        return lax.ppermute(value, "wide", pairs)

    near = [(send(v, -2, every), send(v, 2, every)) for v in own]
    far = [(send(after, -2, every), send(before, 2, second)) for after, before in near]
    streams = []
    for n, (v, (after, before)) in enumerate(zip(own, near)):
        if n == 0:
            before, coeffs = lax.optimization_barrier((before, coeffs))
        streams.append([swap(v), swap(after), swap(before)])
    for n, (v, (after, before), (last, early)) in enumerate(zip(own, near, far)):
        streams[n] = [v, after, before, last] + streams[n] + [send(early, -1, second), send(last, 1, first)]
    return streams, coeffs


def shards(voltages, station_flags, channel_order, beam_stations, beam_weight_re, beam_weight_im):
    _, width, _, length = voltages.shape
    wide, narrow = lax.axis_size("wide"), lax.axis_size("narrow")
    coeffs = held_coefficients(length, wide)
    streams, coeffs = gather_frames([voltages[part, :, 0, :] for part in range(2)], coeffs, wide)
    own_flags = lax.dynamic_slice_in_dim(
        station_flags, lax.axis_index("narrow") * (width // 2), width // 2
    )
    gain = jnp.tile(jnp.repeat(own_flags, 2).astype(jnp.float32), 2)[None, :]
    index = channel_order % OUTER * LANES + channel_order // OUTER
    spectra = channelize(streams[0], streams[1], coeffs, index, gain)
    turned_over = lax.all_to_all(spectra, ("wide", "narrow"), 0, 0, tiled=True)
    voices = turned_over.reshape(wide, narrow, AVG, 2 * width)
    weights = beam_weights(beam_stations, beam_weight_re, beam_weight_im, width * narrow)
    sent = correlate(voices, weights)
    back = lax.all_to_all(sent, "narrow", 0, 0, tiled=True)
    visibilities = back[:, : 2 * width].astype(jnp.float32).reshape(narrow, 2, width, -1)
    beams = beam_stations.shape[0]
    terms = back[:, 2 * width :].astype(jnp.float32).reshape(narrow * AVG, -1)
    energy = terms[:, :beams] + terms[:, beams : 2 * beams] + terms[:, 2 * beams : 3 * beams]
    share = beams // narrow
    beam_power = lax.dynamic_slice_in_dim(energy, lax.axis_index("narrow") * share, share, axis=1)
    return (visibilities, beam_power)


def solution(mesh):
    return jax.shard_map(
        shards,
        mesh=mesh,
        in_specs=(P(None, "narrow", "wide", None), P(), P(), P(), P(), P()),
        out_specs=(P("wide", None, "narrow", None), P("wide", "narrow")),
        check_vma=False,
    )
```

```python
import math

import jax
import jax.numpy as jnp
import numpy as np
from jax import lax
from jax.experimental import pallas as pl
from jax.experimental.pallas import tpu as pltpu
from jax.sharding import PartitionSpec as P

TAPS = 8
AVG = 8
LANES = 128
OUTER = 32
ROWS = 16


LEAD = 4
TAPS_FIRST = (4, 2, 6, 0, 3, 1, 5, 7, TAPS)
TAPS_SECOND = (4, 2, 6, 0, 5, 3, 7, TAPS, 1)
HELD = len(TAPS_FIRST)


def prototype(tap_count, length):
    places = jnp.arange(tap_count * length, dtype=jnp.float32)
    offsets = places / length - tap_count / 2.0
    window = 0.5 - 0.5 * jnp.cos(2.0 * jnp.pi * (places + 0.5) / (tap_count * length))
    return (jnp.sinc(offsets) * window).reshape(tap_count, length)


def fourier_tables():
    length = OUTER * LANES
    inner = np.arange(LANES, dtype=np.float64)
    angle = 2.0 * np.pi * np.arange(OUTER, dtype=np.float64)[:, None] * inner[None, :] / length
    twist = np.stack([np.cos(angle), -np.sin(angle)]).astype(np.float32)
    turn = 2.0 * np.pi * ((np.arange(LANES)[:, None] * np.arange(LANES)[None, :]) % LANES) / LANES
    cos, sin = np.cos(turn), np.sin(turn)
    matrix = (np.block([[cos, -sin], [sin, cos]]) / math.sqrt(length)).astype(np.float32)
    high = matrix.astype(jnp.bfloat16)
    low = (matrix - high.astype(np.float32)).astype(jnp.bfloat16)
    return twist, high, low


def add(a, b):
    return (a[0] + b[0], a[1] + b[1])


def sub(a, b):
    return (a[0] - b[0], a[1] - b[1])


def turned(a, num, den):
    num %= den
    if num == 0:
        return a
    if 4 * num == den:
        return (a[1], -a[0])
    if 2 * num == den:
        return (-a[0], -a[1])
    if 4 * num == 3 * den:
        return (-a[1], a[0])
    cos, sin = math.cos(2.0 * math.pi * num / den), math.sin(2.0 * math.pi * num / den)
    return (a[0] * cos + a[1] * sin, a[1] * cos - a[0] * sin)


def four(x):
    s0, s1, s2, s3 = add(x[0], x[2]), sub(x[0], x[2]), add(x[1], x[3]), sub(x[1], x[3])
    r3 = turned(s3, 1, 4)
    return [add(s0, s2), add(s1, r3), sub(s0, s2), sub(s1, r3)]


def eight(x):
    even, odd = four(x[0::2]), four(x[1::2])
    odd = [turned(odd[q], q, 8) for q in range(4)]
    return [add(even[q], odd[q]) for q in range(4)] + [sub(even[q], odd[q]) for q in range(4)]


def transform_rows(frames_re, frames_im, coeffs, twist, high, low, mid, y_hi, y_lo):
    def filtered(frames, block):
        span = slice(block * LANES, (block + 1) * LANES)
        total = coeffs[0:1, span] * frames[0][:, span].astype(jnp.float32)
        for tap in range(1, HELD):
            total = total + coeffs[tap : tap + 1, span] * frames[tap][:, span].astype(jnp.float32)
        return total

    for j in range(8):
        points = [
            (filtered(frames_re, j + 8 * m), filtered(frames_im, j + 8 * m)) for m in range(4)
        ]
        for p, value in enumerate(four(points)):
            value = turned(value, j * p, OUTER)
            mid[p, j, 0] = value[0]
            mid[p, j, 1] = value[1]
    for p in range(4):
        for q, value in enumerate(eight([(mid[p, j, 0], mid[p, j, 1]) for j in range(8)])):
            c = p + 4 * q
            cos, sin = twist[0, c : c + 1, :], twist[1, c : c + 1, :]
            rows = slice(c * ROWS, (c + 1) * ROWS)
            for part, y in enumerate(
                (value[0] * cos - value[1] * sin, value[0] * sin + value[1] * cos)
            ):
                upper = y.astype(jnp.bfloat16)
                lanes = slice(part * LANES, (part + 1) * LANES)
                y_hi[rows, lanes] = upper
                y_lo[rows, lanes] = (y - upper.astype(jnp.float32)).astype(jnp.bfloat16)

    def dot(a, b):
        return jnp.dot(a[...], b[...], preferred_element_type=jnp.float32)

    return dot(y_hi, high) + (dot(y_lo, high) + dot(y_hi, low))


def early_kernel(*refs):
    coeffs, twist, high, low, spec, mid, y_hi, y_lo = refs[2 * HELD :]
    result = transform_rows(
        refs[:HELD], refs[HELD : 2 * HELD], coeffs, twist, high, low, mid, y_hi, y_lo
    )
    for part in range(2):
        span = slice(part * LANES, (part + 1) * LANES)
        spec[:, part] = result[:, span].reshape(OUTER, ROWS, LANES)


def late_kernel(index, *refs):
    coeffs, twist, high, low, early, gain, out, mid, y_hi, y_lo, spec, lined, picked = refs[2 * HELD :]
    result = transform_rows(
        refs[:HELD], refs[HELD : 2 * HELD], coeffs, twist, high, low, mid, y_hi, y_lo
    )
    for part in range(2):
        span = slice(part * LANES, (part + 1) * LANES)
        spec[:, part] = result[:, span].reshape(OUTER, ROWS, LANES)

    def line(c, carry):
        block = jnp.concatenate([early[c, 0], spec[c, 0], early[c, 1], spec[c, 1]], axis=0)
        lined[pl.ds(pl.multiple_of(c * LANES, LANES), LANES), :] = block.T * gain[...]
        return carry

    lax.fori_loop(0, OUTER, line, 0, unroll=2)
    batch = 32

    def pick(g, carry):
        base = pl.multiple_of(g * batch, batch)
        for j in range(batch):
            picked[pl.ds(base + j, 1), :] = lined[pl.ds(index[base + j], 1), :]
        return carry

    lax.fori_loop(0, OUTER * LANES // batch, pick, 0)
    out[...] = picked[...].reshape(out.shape).astype(jnp.bfloat16)


WORK = [
    pltpu.VMEM((4, 8, 2, ROWS, LANES), jnp.float32),
    pltpu.VMEM((OUTER * ROWS, 2 * LANES), jnp.bfloat16),
    pltpu.VMEM((OUTER * ROWS, 2 * LANES), jnp.bfloat16),
]


def whole(value):
    return pl.BlockSpec(value.shape, lambda *_: (0,) * value.ndim)


def transform_early(frames, coeffs, tables):
    rows, length = frames[0].shape
    steps = rows // 2 // ROWS
    part_re = pl.BlockSpec((ROWS, length), lambda i: (i, 0))
    part_im = pl.BlockSpec((ROWS, length), lambda i: (i + steps, 0))
    return pl.pallas_call(
        early_kernel,
        out_shape=jax.ShapeDtypeStruct((OUTER, 2, rows // 2, LANES), jnp.float32),
        grid_spec=pltpu.PrefetchScalarGridSpec(
            num_scalar_prefetch=0,
            grid=(steps,),
            in_specs=[part_re] * HELD + [part_im] * HELD + [whole(v) for v in (coeffs, *tables)],
            out_specs=pl.BlockSpec((OUTER, 2, ROWS, LANES), lambda i: (0, 0, i, 0)),
            scratch_shapes=WORK,
        ),
        compiler_params=pltpu.CompilerParams(dimension_semantics=("arbitrary",)),
        name="transform_early",
    )(*frames, *frames, coeffs, *tables)


def transform_late(frames, coeffs, tables, early, index, gain):
    length = frames[0].shape[1]
    width = gain.shape[1]
    part_re = pl.BlockSpec((ROWS, length), lambda i, idx: (0, 0))
    part_im = pl.BlockSpec((ROWS, length), lambda i, idx: (1, 0))
    return pl.pallas_call(
        late_kernel,
        out_shape=jax.ShapeDtypeStruct((length // AVG, AVG, width), jnp.bfloat16),
        grid_spec=pltpu.PrefetchScalarGridSpec(
            num_scalar_prefetch=1,
            grid=(1,),
            in_specs=[part_re] * HELD
            + [part_im] * HELD
            + [whole(v) for v in (coeffs, *tables, early, gain)],
            out_specs=pl.BlockSpec((length // AVG, AVG, width), lambda i, idx: (0, 0, 0)),
            scratch_shapes=WORK
            + [
                pltpu.VMEM((OUTER, 2, ROWS, LANES), jnp.float32),
                pltpu.VMEM((length, width), jnp.float32),
                pltpu.VMEM((length, width), jnp.float32),
            ],
        ),
        compiler_params=pltpu.CompilerParams(dimension_semantics=("arbitrary",)),
        name="transform_late",
    )(index, *frames, *frames, coeffs, *tables, early, gain)


def weights_kernel(stations, weight_re, weight_im, out):
    inputs = out.shape[0] // 2
    beams = stations.shape[1]
    chunk = 64

    def block(n, carry):
        start = pl.multiple_of(n * chunk, chunk)
        rows = lax.broadcasted_iota(jnp.int32, (chunk, beams), 0) + start
        station = rows // 2

        def pick(t, sums):
            here = stations[pl.ds(t, 1), :] == station
            return (
                sums[0] + jnp.where(here, weight_re[pl.ds(t, 1), :], 0.0),
                sums[1] + jnp.where(here, weight_im[pl.ds(t, 1), :], 0.0),
            )

        zero = jnp.zeros((chunk, beams), jnp.float32)
        sum_re, sum_im = lax.fori_loop(0, stations.shape[0], pick, (zero, zero), unroll=4)
        for pol in range(2):
            own = rows % 2 == pol
            part_re = jnp.where(own, sum_re, 0.0).astype(jnp.bfloat16)
            part_im = jnp.where(own, sum_im, 0.0).astype(jnp.bfloat16)
            first = slice(2 * pol * beams, (2 * pol + 1) * beams)
            second = slice((2 * pol + 1) * beams, (2 * pol + 2) * beams)
            out[pl.ds(start, chunk), first] = part_re
            out[pl.ds(start, chunk), second] = part_im
            out[pl.ds(inputs + start, chunk), first] = -part_im
            out[pl.ds(inputs + start, chunk), second] = part_re
        return carry

    lax.fori_loop(0, inputs // chunk, block, 0)


def beam_weights(beam_stations, weight_re, weight_im, input_count):
    beams = beam_stations.shape[0]
    return pl.pallas_call(
        weights_kernel,
        out_shape=jax.ShapeDtypeStruct((2 * input_count, 4 * beams), jnp.bfloat16),
        name="beam_weights",
    )(beam_stations.T, weight_re.T, weight_im.T)


def correlate_kernel(voices, weights, out, x_ref, xt_ref):
    frames, groups, avg, width = voices.shape
    half = width // 2
    count = groups * half
    depth = frames * avg
    lane = lax.broadcasted_iota(jnp.int32, (depth, width), 1)
    for m in range(groups // 2):
        a = voices[:, 2 * m].astype(jnp.float32).reshape(depth, width)
        b = voices[:, 2 * m + 1].astype(jnp.float32).reshape(depth, width)
        re = jnp.where(lane < half, a, pltpu.roll(b, half, 1))
        im = jnp.where(lane < half, pltpu.roll(a, half, 1), b)
        for part, value in enumerate((re, im)):
            span = slice(part * count + m * width, part * count + (m + 1) * width)
            x_ref[:, span] = value.astype(jnp.bfloat16)
            xt_ref[span, :] = value.T.astype(jnp.bfloat16)

    def dot(a, b):
        return jnp.dot(a, b, preferred_element_type=jnp.float32)

    power = dot(x_ref[...], weights[...])
    power = power * power
    beams = power.shape[1] // 4
    energy = power[:, :beams] + power[:, beams : 2 * beams]
    energy = energy + (power[:, 2 * beams : 3 * beams] + power[:, 3 * beams :])
    energy = jnp.sum(energy.reshape(frames, avg, beams), axis=0) / frames
    first = energy.astype(jnp.bfloat16)
    rest = energy - first.astype(jnp.float32)
    second = rest.astype(jnp.bfloat16)
    third = (rest - second.astype(jnp.float32)).astype(jnp.bfloat16)
    terms = jnp.concatenate([first, second, third, jnp.zeros_like(first)], axis=1)

    scale = 1.0 / math.sqrt(depth)
    x_re, x_im = x_ref[:, :count], x_ref[:, count:]
    for r in range(groups):
        xt_re = xt_ref[r * half : (r + 1) * half, :]
        xt_im = xt_ref[count + r * half : count + (r + 1) * half, :]
        out[r, :half, :] = ((dot(xt_re, x_re) + dot(xt_im, x_im)) * scale).astype(jnp.bfloat16)
        out[r, half:width, :] = ((dot(xt_im, x_re) - dot(xt_re, x_im)) * scale).astype(jnp.bfloat16)
        out[r, width:, :] = terms


def correlate(voices, weights):
    frames, groups, avg, width = voices.shape
    count = groups * width // 2
    depth = frames * avg
    return pl.pallas_call(
        correlate_kernel,
        out_shape=jax.ShapeDtypeStruct((groups, width + avg, count), jnp.bfloat16),
        scratch_shapes=[
            pltpu.VMEM((depth, 2 * count), jnp.bfloat16),
            pltpu.VMEM((2 * count, depth), jnp.bfloat16),
        ],
        name="correlate",
    )(voices, weights)


def held_coefficients(length, wide):
    place = lax.axis_index("wide")
    frame = (place + LEAD) % wide
    taps = jnp.where(place % 2 == 0, jnp.array(TAPS_FIRST), jnp.array(TAPS_SECOND))
    picked = taps[:, None] == jnp.arange(TAPS)[None, :]
    used = jnp.logical_and(picked, (taps <= frame)[:, None])
    table = prototype(TAPS, length)
    rows = [jnp.where(used[:, tap, None], table[tap], 0.0) for tap in range(TAPS)]
    return sum(rows[1:], rows[0])


def gather_frames(own, beside, wide):
    def send(value, step, places):
        return lax.ppermute(value, "wide", [(d, (d + step) % wide) for d in places])

    every, first, second = range(wide), range(0, wide, 2), range(1, wide, 2)

    def swap(value):
        pairs = [(d, d ^ 1) for d in every]
        return lax.ppermute(value, "wide", pairs)

    near = [(send(v, -2, every), send(v, 2, every)) for v in own]
    far = [(send(after, -2, every), send(before, 2, second)) for after, before in near]
    streams = []
    for n, (v, (after, before)) in enumerate(zip(own, near)):
        if n == 0:
            before, beside = lax.optimization_barrier((before, beside))
        streams.append([swap(v), swap(after), swap(before)])
    for n, (v, (after, before), (last, early)) in enumerate(zip(own, near, far)):
        streams[n] = [v, after, before, last] + streams[n] + [send(early, -1, second), send(last, 1, first)]
    return streams, beside


def shards(voltages, station_flags, channel_order, beam_stations, beam_weight_re, beam_weight_im):
    _, width, _, length = voltages.shape
    wide, narrow = lax.axis_size("wide"), lax.axis_size("narrow")
    beside = (
        held_coefficients(length, wide),
        beam_weights(beam_stations, beam_weight_re, beam_weight_im, width * narrow),
    )
    cut = width - ROWS
    own = [
        voltages[:, :cut, 0, :].reshape(2 * cut, length),
        voltages[:, cut:, 0, :].reshape(2 * ROWS, length),
    ]
    streams, (coeffs, weights) = gather_frames(own, beside, wide)

    own_flags = lax.dynamic_slice_in_dim(
        station_flags, lax.axis_index("narrow") * (width // 2), width // 2
    )
    gain = jnp.tile(jnp.repeat(own_flags, 2).astype(jnp.float32), 2)[None, :]
    index = channel_order % OUTER * LANES + channel_order // OUTER
    tables = [jnp.asarray(table) for table in fourier_tables()]
    early = transform_early(streams[0], coeffs, tables)
    spectra = transform_late(streams[1], coeffs, tables, early, index, gain)
    turned_over = lax.all_to_all(spectra, ("wide", "narrow"), 0, 0, tiled=True)
    voices = turned_over.reshape(wide, narrow, AVG, 2 * width)
    sent = correlate(voices, weights)
    back = lax.all_to_all(sent, "narrow", 0, 0, tiled=True)
    visibilities = back[:, : 2 * width].astype(jnp.float32).reshape(narrow, 2, width, -1)
    beams = beam_stations.shape[0]
    terms = back[:, 2 * width :].astype(jnp.float32).reshape(narrow * AVG, -1)
    energy = terms[:, :beams] + terms[:, beams : 2 * beams] + terms[:, 2 * beams : 3 * beams]
    share = beams // narrow
    beam_power = lax.dynamic_slice_in_dim(energy, lax.axis_index("narrow") * share, share, axis=1)
    return (visibilities, beam_power)


def solution(mesh):
    return jax.shard_map(
        shards,
        mesh=mesh,
        in_specs=(P(None, "narrow", "wide", None), P(), P(), P(), P(), P()),
        out_specs=(P("wide", None, "narrow", None), P("wide", "narrow")),
        check_vma=False,
    )
```

```python
import math

import jax
import jax.numpy as jnp
import numpy as np
from jax import lax
from jax.experimental import pallas as pl
from jax.experimental.pallas import tpu as pltpu
from jax.sharding import PartitionSpec as P

TAPS = 8
AVG = 8
LANES = 128
OUTER = 32
ROWS = 16


LEAD = 4
TAPS_FIRST = (4, 2, 6, 3, 1, 5, 7, 0, TAPS, TAPS)
TAPS_SECOND = (4, 2, 6, 5, 3, 7, TAPS, TAPS, 0, 1)
HELD = len(TAPS_FIRST)


def prototype(tap_count, length):
    places = jnp.arange(tap_count * length, dtype=jnp.float32)
    offsets = places / length - tap_count / 2.0
    window = 0.5 - 0.5 * jnp.cos(2.0 * jnp.pi * (places + 0.5) / (tap_count * length))
    return (jnp.sinc(offsets) * window).reshape(tap_count, length)


def fourier_tables():
    length = OUTER * LANES
    inner = np.arange(LANES, dtype=np.float64)
    angle = 2.0 * np.pi * np.arange(OUTER, dtype=np.float64)[:, None] * inner[None, :] / length
    twist = np.stack([np.cos(angle), -np.sin(angle)]).astype(np.float32)
    turn = 2.0 * np.pi * ((np.arange(LANES)[:, None] * np.arange(LANES)[None, :]) % LANES) / LANES
    cos, sin = np.cos(turn), np.sin(turn)
    matrix = (np.block([[cos, -sin], [sin, cos]]) / math.sqrt(length)).astype(np.float32)
    high = matrix.astype(jnp.bfloat16)
    low = (matrix - high.astype(np.float32)).astype(jnp.bfloat16)
    return twist, high, low


def add(a, b):
    return (a[0] + b[0], a[1] + b[1])


def sub(a, b):
    return (a[0] - b[0], a[1] - b[1])


def turned(a, num, den):
    num %= den
    if num == 0:
        return a
    if 4 * num == den:
        return (a[1], -a[0])
    if 2 * num == den:
        return (-a[0], -a[1])
    if 4 * num == 3 * den:
        return (-a[1], a[0])
    cos, sin = math.cos(2.0 * math.pi * num / den), math.sin(2.0 * math.pi * num / den)
    return (a[0] * cos + a[1] * sin, a[1] * cos - a[0] * sin)


def four(x):
    s0, s1, s2, s3 = add(x[0], x[2]), sub(x[0], x[2]), add(x[1], x[3]), sub(x[1], x[3])
    r3 = turned(s3, 1, 4)
    return [add(s0, s2), add(s1, r3), sub(s0, s2), sub(s1, r3)]


def eight(x):
    even, odd = four(x[0::2]), four(x[1::2])
    odd = [turned(odd[q], q, 8) for q in range(4)]
    return [add(even[q], odd[q]) for q in range(4)] + [sub(even[q], odd[q]) for q in range(4)]


def channelize_kernel(index, *refs):
    frames_re, frames_im = refs[:HELD], refs[HELD : 2 * HELD]
    coeffs, twist, high, low, gain, out, mid, y_hi, y_lo, spec, lined, picked = refs[2 * HELD :]
    step = pl.program_id(0)

    def filtered(frames, block):
        span = slice(block * LANES, (block + 1) * LANES)
        total = coeffs[0:1, span] * frames[0][:, span].astype(jnp.float32)
        for tap in range(1, HELD):
            total = total + coeffs[tap : tap + 1, span] * frames[tap][:, span].astype(jnp.float32)
        return total

    for j in range(8):
        points = [
            (filtered(frames_re, j + 8 * m), filtered(frames_im, j + 8 * m)) for m in range(4)
        ]
        for p, value in enumerate(four(points)):
            value = turned(value, j * p, OUTER)
            mid[p, j, 0] = value[0]
            mid[p, j, 1] = value[1]
    for p in range(4):
        for q, value in enumerate(eight([(mid[p, j, 0], mid[p, j, 1]) for j in range(8)])):
            c = p + 4 * q
            cos, sin = twist[0, c : c + 1, :], twist[1, c : c + 1, :]
            rows = slice(c * ROWS, (c + 1) * ROWS)
            for part, y in enumerate(
                (value[0] * cos - value[1] * sin, value[0] * sin + value[1] * cos)
            ):
                upper = y.astype(jnp.bfloat16)
                lanes = slice(part * LANES, (part + 1) * LANES)
                y_hi[rows, lanes] = upper
                y_lo[rows, lanes] = (y - upper.astype(jnp.float32)).astype(jnp.bfloat16)

    def dot(a, b):
        return jnp.dot(a[...], b[...], preferred_element_type=jnp.float32)

    result = dot(y_hi, high) + (dot(y_lo, high) + dot(y_hi, low))
    start = pl.multiple_of(step * ROWS, ROWS)
    for part in range(2):
        spec[:, part, pl.ds(start, ROWS), :] = result[:, part * LANES : (part + 1) * LANES].reshape(
            OUTER, ROWS, LANES
        )

    @pl.when(step == pl.num_programs(0) - 1)
    def _():
        width = spec.shape[2]

        def line(c, carry):
            block = spec[c].reshape(2 * width, LANES)
            rows = pl.ds(pl.multiple_of(c * LANES, LANES), LANES)
            lined[rows, :] = block.astype(jnp.bfloat16).T.astype(jnp.float32) * gain[...]
            return carry

        lax.fori_loop(0, OUTER, line, 0, unroll=4)
        batch = 64

        def pick(g, carry):
            base = pl.multiple_of(g * batch, batch)
            for j in range(batch):
                picked[pl.ds(base + j, 1), :] = lined[pl.ds(index[base + j], 1), :]
            return carry

        lax.fori_loop(0, OUTER * LANES // batch, pick, 0)
        out[...] = picked[...].reshape(out.shape).astype(jnp.bfloat16)


def channelize(frames_re, frames_im, coeffs, index, gain):
    width, length = frames_re[0].shape
    twist, high, low = fourier_tables()
    frame = pl.BlockSpec((ROWS, length), lambda i, idx: (i, 0))

    def whole(shape):
        return pl.BlockSpec(shape, lambda i, idx: (0,) * len(shape))

    return pl.pallas_call(
        channelize_kernel,
        out_shape=jax.ShapeDtypeStruct((length // AVG, AVG, 2 * width), jnp.bfloat16),
        grid_spec=pltpu.PrefetchScalarGridSpec(
            num_scalar_prefetch=1,
            grid=(width // ROWS,),
            in_specs=[frame] * (2 * HELD)
            + [whole(coeffs.shape), whole(twist.shape), whole(high.shape), whole(low.shape)]
            + [whole(gain.shape)],
            out_specs=whole((length // AVG, AVG, 2 * width)),
            scratch_shapes=[
                pltpu.VMEM((4, 8, 2, ROWS, LANES), jnp.float32),
                pltpu.VMEM((OUTER * ROWS, 2 * LANES), jnp.bfloat16),
                pltpu.VMEM((OUTER * ROWS, 2 * LANES), jnp.bfloat16),
                pltpu.VMEM((OUTER, 2, width, LANES), jnp.float32),
                pltpu.VMEM((length, 2 * width), jnp.float32),
                pltpu.VMEM((length, 2 * width), jnp.float32),
            ],
        ),
        compiler_params=pltpu.CompilerParams(dimension_semantics=("arbitrary",)),
        name="channelize",
    )(index, *frames_re, *frames_im, coeffs, jnp.asarray(twist), jnp.asarray(high), jnp.asarray(low), gain)


def weights_kernel(stations, weight_re, weight_im, out):
    inputs = out.shape[0] // 2
    beams = stations.shape[1]
    chunk = 64

    def block(n, carry):
        start = pl.multiple_of(n * chunk, chunk)
        rows = lax.broadcasted_iota(jnp.int32, (chunk, beams), 0) + start
        station = rows // 2

        def pick(t, sums):
            here = stations[pl.ds(t, 1), :] == station
            return (
                sums[0] + jnp.where(here, weight_re[pl.ds(t, 1), :], 0.0),
                sums[1] + jnp.where(here, weight_im[pl.ds(t, 1), :], 0.0),
            )

        zero = jnp.zeros((chunk, beams), jnp.float32)
        sum_re, sum_im = lax.fori_loop(0, stations.shape[0], pick, (zero, zero), unroll=4)
        for pol in range(2):
            own = rows % 2 == pol
            part_re = jnp.where(own, sum_re, 0.0).astype(jnp.bfloat16)
            part_im = jnp.where(own, sum_im, 0.0).astype(jnp.bfloat16)
            first = slice(2 * pol * beams, (2 * pol + 1) * beams)
            second = slice((2 * pol + 1) * beams, (2 * pol + 2) * beams)
            out[pl.ds(start, chunk), first] = part_re
            out[pl.ds(start, chunk), second] = part_im
            out[pl.ds(inputs + start, chunk), first] = -part_im
            out[pl.ds(inputs + start, chunk), second] = part_re
        return carry

    lax.fori_loop(0, inputs // chunk, block, 0)


def beam_weights(beam_stations, weight_re, weight_im, input_count):
    beams = beam_stations.shape[0]
    return pl.pallas_call(
        weights_kernel,
        out_shape=jax.ShapeDtypeStruct((2 * input_count, 4 * beams), jnp.bfloat16),
        name="beam_weights",
    )(beam_stations.T, weight_re.T, weight_im.T)


def correlate_kernel(voices, weights, out, x_ref, xt_ref):
    frames, groups, avg, width = voices.shape
    half = width // 2
    count = groups * half
    depth = frames * avg
    lane = lax.broadcasted_iota(jnp.int32, (depth, width), 1)
    for m in range(groups // 2):
        a = voices[:, 2 * m].astype(jnp.float32).reshape(depth, width)
        b = voices[:, 2 * m + 1].astype(jnp.float32).reshape(depth, width)
        re = jnp.where(lane < half, a, pltpu.roll(b, half, 1))
        im = jnp.where(lane < half, pltpu.roll(a, half, 1), b)
        for part, value in enumerate((re, im)):
            span = slice(part * count + m * width, part * count + (m + 1) * width)
            x_ref[:, span] = value.astype(jnp.bfloat16)
            xt_ref[span, :] = value.T.astype(jnp.bfloat16)

    def dot(a, b):
        return jnp.dot(a, b, preferred_element_type=jnp.float32)

    power = dot(x_ref[...], weights[...])
    power = power * power
    beams = power.shape[1] // 4
    energy = power[:, :beams] + power[:, beams : 2 * beams]
    energy = energy + (power[:, 2 * beams : 3 * beams] + power[:, 3 * beams :])
    energy = jnp.sum(energy.reshape(frames, avg, beams), axis=0) / frames
    first = energy.astype(jnp.bfloat16)
    rest = energy - first.astype(jnp.float32)
    second = rest.astype(jnp.bfloat16)
    third = (rest - second.astype(jnp.float32)).astype(jnp.bfloat16)
    terms = jnp.concatenate([first, second, third, jnp.zeros_like(first)], axis=1)

    scale = 1.0 / math.sqrt(depth)
    x_re, x_im = x_ref[:, :count], x_ref[:, count:]
    for r in range(groups):
        xt_re = xt_ref[r * half : (r + 1) * half, :]
        xt_im = xt_ref[count + r * half : count + (r + 1) * half, :]
        out[r, :half, :] = ((dot(xt_re, x_re) + dot(xt_im, x_im)) * scale).astype(jnp.bfloat16)
        out[r, half:width, :] = ((dot(xt_im, x_re) - dot(xt_re, x_im)) * scale).astype(jnp.bfloat16)
        out[r, width:, :] = terms


def correlate(voices, weights):
    frames, groups, avg, width = voices.shape
    count = groups * width // 2
    depth = frames * avg
    return pl.pallas_call(
        correlate_kernel,
        out_shape=jax.ShapeDtypeStruct((groups, width + avg, count), jnp.bfloat16),
        scratch_shapes=[
            pltpu.VMEM((depth, 2 * count), jnp.bfloat16),
            pltpu.VMEM((2 * count, depth), jnp.bfloat16),
        ],
        name="correlate",
    )(voices, weights)


def held_coefficients(length, wide):
    place = lax.axis_index("wide")
    frame = (place + LEAD) % wide
    taps = jnp.where(place % 2 == 0, jnp.array(TAPS_FIRST), jnp.array(TAPS_SECOND))
    picked = taps[:, None] == jnp.arange(TAPS)[None, :]
    used = jnp.logical_and(picked, (taps <= frame)[:, None])
    table = prototype(TAPS, length)
    rows = [jnp.where(used[:, tap, None], table[tap], 0.0) for tap in range(TAPS)]
    return sum(rows[1:], rows[0])


def gather_frames(own, beside, wide):
    def send(value, step, places):
        return lax.ppermute(value, "wide", [(d, (d + step) % wide) for d in places])

    every, first, second = range(wide), range(0, wide, 2), range(1, wide, 2)

    def swap(value):
        pairs = [(d, d ^ 1) for d in every]
        return lax.ppermute(value, "wide", pairs)

    near = [(send(v, -2, every), send(v, 2, every)) for v in own]
    near[0], beside = lax.optimization_barrier((near[0], beside))
    streams = []
    for v, (after, before) in zip(own, near):
        last = send(after, -2, first)
        streams.append([v, after, before, send(before, 1, second), last, send(after, -2, second)])
    for n, (v, after, before, early, last_first, last_second) in enumerate(streams):
        shared = [swap(v), swap(after), swap(before)]
        streams[n] = [v, after, before] + shared + [early, last_first, last_second]
        streams[n].append(send(last_first, 1, first))
    return streams, beside


def shards(voltages, station_flags, channel_order, beam_stations, beam_weight_re, beam_weight_im):
    _, width, _, length = voltages.shape
    wide, narrow = lax.axis_size("wide"), lax.axis_size("narrow")
    beside = (
        held_coefficients(length, wide),
        beam_weights(beam_stations, beam_weight_re, beam_weight_im, width * narrow),
    )
    own = [voltages[part, :, 0, :] for part in range(2)]
    streams, (coeffs, weights) = gather_frames(own, beside, wide)
    own_flags = lax.dynamic_slice_in_dim(
        station_flags, lax.axis_index("narrow") * (width // 2), width // 2
    )
    gain = jnp.tile(jnp.repeat(own_flags, 2).astype(jnp.float32), 2)[None, :]
    index = channel_order % OUTER * LANES + channel_order // OUTER
    spectra = channelize(streams[0], streams[1], coeffs, index, gain)
    turned_over = lax.all_to_all(spectra, ("wide", "narrow"), 0, 0, tiled=True)
    voices = turned_over.reshape(wide, narrow, AVG, 2 * width)
    sent = correlate(voices, weights)
    back = lax.all_to_all(sent, "narrow", 0, 0, tiled=True)
    visibilities = back[:, : 2 * width].astype(jnp.float32).reshape(narrow, 2, width, -1)
    beams = beam_stations.shape[0]
    terms = back[:, 2 * width :].astype(jnp.float32).reshape(narrow * AVG, -1)
    energy = terms[:, :beams] + terms[:, beams : 2 * beams] + terms[:, 2 * beams : 3 * beams]
    share = beams // narrow
    beam_power = lax.dynamic_slice_in_dim(energy, lax.axis_index("narrow") * share, share, axis=1)
    return (visibilities, beam_power)


def solution(mesh):
    return jax.shard_map(
        shards,
        mesh=mesh,
        in_specs=(P(None, "narrow", "wide", None), P(), P(), P(), P(), P()),
        out_specs=(P("wide", None, "narrow", None), P("wide", "narrow")),
        check_vma=False,
    )
```

```python
import math

import jax
import jax.numpy as jnp
import numpy as np
from jax import lax
from jax.experimental import pallas as pl
from jax.experimental.pallas import tpu as pltpu
from jax.sharding import PartitionSpec as P


TAPS = 8
AVG = 8
LANES = 128
OUTER = 32
ROWS = 16


LEAD = 4
TAPS_FIRST = (4, 2, 6, 0, 3, 1, 5, 7, TAPS)
TAPS_SECOND = (4, 2, 6, 0, 5, 3, 7, TAPS, 1)
HELD = len(TAPS_FIRST)


def prototype(tap_count, length):
    places = jnp.arange(tap_count * length, dtype=jnp.float32)
    offsets = places / length - tap_count / 2.0
    window = 0.5 - 0.5 * jnp.cos(2.0 * jnp.pi * (places + 0.5) / (tap_count * length))
    return (jnp.sinc(offsets) * window).reshape(tap_count, length)


def fourier_tables():
    length = OUTER * LANES
    inner = np.arange(LANES, dtype=np.float64)
    angle = 2.0 * np.pi * np.arange(OUTER, dtype=np.float64)[:, None] * inner[None, :] / length
    twist = np.stack([np.cos(angle), -np.sin(angle)]).astype(np.float32)
    turn = 2.0 * np.pi * ((np.arange(LANES)[:, None] * np.arange(LANES)[None, :]) % LANES) / LANES
    cos, sin = np.cos(turn), np.sin(turn)
    matrix = (np.block([[cos, -sin], [sin, cos]]) / math.sqrt(length)).astype(np.float32)
    high = matrix.astype(jnp.bfloat16)
    low = (matrix - high.astype(np.float32)).astype(jnp.bfloat16)
    return twist, high, low


def add(a, b):
    return (a[0] + b[0], a[1] + b[1])


def sub(a, b):
    return (a[0] - b[0], a[1] - b[1])


def turned(a, num, den):
    num %= den
    if num == 0:
        return a
    if 4 * num == den:
        return (a[1], -a[0])
    if 2 * num == den:
        return (-a[0], -a[1])
    if 4 * num == 3 * den:
        return (-a[1], a[0])
    cos, sin = math.cos(2.0 * math.pi * num / den), math.sin(2.0 * math.pi * num / den)
    return (a[0] * cos + a[1] * sin, a[1] * cos - a[0] * sin)


def four(x):
    s0, s1, s2, s3 = add(x[0], x[2]), sub(x[0], x[2]), add(x[1], x[3]), sub(x[1], x[3])
    r3 = turned(s3, 1, 4)
    return [add(s0, s2), add(s1, r3), sub(s0, s2), sub(s1, r3)]


def eight(x):
    even, odd = four(x[0::2]), four(x[1::2])
    odd = [turned(odd[q], q, 8) for q in range(4)]
    return [add(even[q], odd[q]) for q in range(4)] + [sub(even[q], odd[q]) for q in range(4)]


def channelize_kernel(index, *refs):
    frames_re, frames_im = refs[:HELD], refs[HELD : 2 * HELD]
    coeffs, twist, high, low, gain, out, mid, y_hi, y_lo, spec, lined, picked = refs[2 * HELD :]
    step = pl.program_id(0)

    def filtered(frames, block):
        span = slice(block * LANES, (block + 1) * LANES)
        total = coeffs[0:1, span] * frames[0][:, span].astype(jnp.float32)
        for tap in range(1, HELD):
            total = total + coeffs[tap : tap + 1, span] * frames[tap][:, span].astype(jnp.float32)
        return total

    for j in range(8):
        points = [
            (filtered(frames_re, j + 8 * m), filtered(frames_im, j + 8 * m)) for m in range(4)
        ]
        for p, value in enumerate(four(points)):
            value = turned(value, j * p, OUTER)
            mid[p, j, 0] = value[0]
            mid[p, j, 1] = value[1]
    for p in range(4):
        for q, value in enumerate(eight([(mid[p, j, 0], mid[p, j, 1]) for j in range(8)])):
            c = p + 4 * q
            cos, sin = twist[0, c : c + 1, :], twist[1, c : c + 1, :]
            rows = slice(c * ROWS, (c + 1) * ROWS)
            for part, y in enumerate(
                (value[0] * cos - value[1] * sin, value[0] * sin + value[1] * cos)
            ):
                upper = y.astype(jnp.bfloat16)
                lanes = slice(part * LANES, (part + 1) * LANES)
                y_hi[rows, lanes] = upper
                y_lo[rows, lanes] = (y - upper.astype(jnp.float32)).astype(jnp.bfloat16)

    def dot(a, b):
        return jnp.dot(a[...], b[...], preferred_element_type=jnp.float32)

    result = dot(y_hi, high) + (dot(y_lo, high) + dot(y_hi, low))
    start = pl.multiple_of(step * ROWS, ROWS)
    for part in range(2):
        spec[:, part, pl.ds(start, ROWS), :] = result[:, part * LANES : (part + 1) * LANES].reshape(
            OUTER, ROWS, LANES
        )

    @pl.when(step == pl.num_programs(0) - 1)
    def _():
        width = spec.shape[2]

        def line(c, carry):
            block = spec[c].reshape(2 * width, LANES)
            rows = pl.ds(pl.multiple_of(c * LANES, LANES), LANES)
            lined[rows, :] = block.astype(jnp.bfloat16).T.astype(jnp.float32) * gain[...]
            return carry

        lax.fori_loop(0, OUTER, line, 0, unroll=4)
        batch = 64

        def pick(g, carry):
            base = pl.multiple_of(g * batch, batch)
            for j in range(batch):
                picked[pl.ds(base + j, 1), :] = lined[pl.ds(index[base + j], 1), :]
            return carry

        lax.fori_loop(0, OUTER * LANES // batch, pick, 0)
        out[...] = picked[...].reshape(out.shape).astype(jnp.bfloat16)


def channelize(frames_re, frames_im, coeffs, index, gain):
    width, length = frames_re[0].shape
    twist, high, low = fourier_tables()
    frame = pl.BlockSpec((ROWS, length), lambda i, idx: (i, 0))

    def whole(shape):
        return pl.BlockSpec(shape, lambda i, idx: (0,) * len(shape))

    return pl.pallas_call(
        channelize_kernel,
        out_shape=jax.ShapeDtypeStruct((length // AVG, AVG, 2 * width), jnp.bfloat16),
        grid_spec=pltpu.PrefetchScalarGridSpec(
            num_scalar_prefetch=1,
            grid=(width // ROWS,),
            in_specs=[frame] * (2 * HELD)
            + [whole(coeffs.shape), whole(twist.shape), whole(high.shape), whole(low.shape)]
            + [whole(gain.shape)],
            out_specs=whole((length // AVG, AVG, 2 * width)),
            scratch_shapes=[
                pltpu.VMEM((4, 8, 2, ROWS, LANES), jnp.float32),
                pltpu.VMEM((OUTER * ROWS, 2 * LANES), jnp.bfloat16),
                pltpu.VMEM((OUTER * ROWS, 2 * LANES), jnp.bfloat16),
                pltpu.VMEM((OUTER, 2, width, LANES), jnp.float32),
                pltpu.VMEM((length, 2 * width), jnp.float32),
                pltpu.VMEM((length, 2 * width), jnp.float32),
            ],
        ),
        compiler_params=pltpu.CompilerParams(dimension_semantics=("arbitrary",)),
        name="channelize",
    )(index, *frames_re, *frames_im, coeffs, jnp.asarray(twist), jnp.asarray(high), jnp.asarray(low), gain)


def weights_kernel(stations, weight_re, weight_im, out):
    inputs = out.shape[0] // 2
    beams = stations.shape[1]
    chunk = 64

    def block(n, carry):
        start = pl.multiple_of(n * chunk, chunk)
        rows = lax.broadcasted_iota(jnp.int32, (chunk, beams), 0) + start
        station = rows // 2

        def pick(t, sums):
            here = stations[pl.ds(t, 1), :] == station
            return (
                sums[0] + jnp.where(here, weight_re[pl.ds(t, 1), :], 0.0),
                sums[1] + jnp.where(here, weight_im[pl.ds(t, 1), :], 0.0),
            )

        zero = jnp.zeros((chunk, beams), jnp.float32)
        sum_re, sum_im = lax.fori_loop(0, stations.shape[0], pick, (zero, zero), unroll=4)
        for pol in range(2):
            own = rows % 2 == pol
            part_re = jnp.where(own, sum_re, 0.0).astype(jnp.bfloat16)
            part_im = jnp.where(own, sum_im, 0.0).astype(jnp.bfloat16)
            first = slice(2 * pol * beams, (2 * pol + 1) * beams)
            second = slice((2 * pol + 1) * beams, (2 * pol + 2) * beams)
            out[pl.ds(start, chunk), first] = part_re
            out[pl.ds(start, chunk), second] = part_im
            out[pl.ds(inputs + start, chunk), first] = -part_im
            out[pl.ds(inputs + start, chunk), second] = part_re
        return carry

    lax.fori_loop(0, inputs // chunk, block, 0)


def beam_weights(beam_stations, weight_re, weight_im, input_count):
    beams = beam_stations.shape[0]
    return pl.pallas_call(
        weights_kernel,
        out_shape=jax.ShapeDtypeStruct((2 * input_count, 4 * beams), jnp.bfloat16),
        name="beam_weights",
    )(beam_stations.T, weight_re.T, weight_im.T)


def correlate_kernel(voices, weights, out, x_ref, xt_ref):
    frames, groups, avg, width = voices.shape
    half = width // 2
    count = groups * half
    depth = frames * avg
    lane = lax.broadcasted_iota(jnp.int32, (depth, width), 1)
    for m in range(groups // 2):
        a = voices[:, 2 * m].astype(jnp.float32).reshape(depth, width)
        b = voices[:, 2 * m + 1].astype(jnp.float32).reshape(depth, width)
        re = jnp.where(lane < half, a, pltpu.roll(b, half, 1))
        im = jnp.where(lane < half, pltpu.roll(a, half, 1), b)
        for part, value in enumerate((re, im)):
            span = slice(part * count + m * width, part * count + (m + 1) * width)
            x_ref[:, span] = value.astype(jnp.bfloat16)
            xt_ref[span, :] = value.T.astype(jnp.bfloat16)

    def dot(a, b):
        return jnp.dot(a, b, preferred_element_type=jnp.float32)

    power = dot(x_ref[...], weights[...])
    power = power * power
    beams = power.shape[1] // 4
    energy = power[:, :beams] + power[:, beams : 2 * beams]
    energy = energy + (power[:, 2 * beams : 3 * beams] + power[:, 3 * beams :])
    energy = jnp.sum(energy.reshape(frames, avg, beams), axis=0) / frames
    first = energy.astype(jnp.bfloat16)
    rest = energy - first.astype(jnp.float32)
    second = rest.astype(jnp.bfloat16)
    third = (rest - second.astype(jnp.float32)).astype(jnp.bfloat16)
    terms = jnp.concatenate([first, second, third, jnp.zeros_like(first)], axis=1)

    scale = 1.0 / math.sqrt(depth)
    x_re, x_im = x_ref[:, :count], x_ref[:, count:]
    for r in range(groups):
        xt_re = xt_ref[r * half : (r + 1) * half, :]
        xt_im = xt_ref[count + r * half : count + (r + 1) * half, :]
        out[r, :half, :] = ((dot(xt_re, x_re) + dot(xt_im, x_im)) * scale).astype(jnp.bfloat16)
        out[r, half:width, :] = ((dot(xt_im, x_re) - dot(xt_re, x_im)) * scale).astype(jnp.bfloat16)
        out[r, width:, :] = terms


def correlate(voices, weights):
    frames, groups, avg, width = voices.shape
    count = groups * width // 2
    depth = frames * avg
    return pl.pallas_call(
        correlate_kernel,
        out_shape=jax.ShapeDtypeStruct((groups, width + avg, count), jnp.bfloat16),
        scratch_shapes=[
            pltpu.VMEM((depth, 2 * count), jnp.bfloat16),
            pltpu.VMEM((2 * count, depth), jnp.bfloat16),
        ],
        name="correlate",
    )(voices, weights)


def held_coefficients(length, wide):
    place = lax.axis_index("wide")
    frame = (place + LEAD) % wide
    taps = jnp.where(place % 2 == 0, jnp.array(TAPS_FIRST), jnp.array(TAPS_SECOND))
    picked = taps[:, None] == jnp.arange(TAPS)[None, :]
    used = jnp.logical_and(picked, (taps <= frame)[:, None])
    table = prototype(TAPS, length)
    rows = [jnp.where(used[:, tap, None], table[tap], 0.0) for tap in range(TAPS)]
    return sum(rows[1:], rows[0])


def gather_frames(own, coeffs, wide):
    def send(value, step, places):
        return lax.ppermute(value, "wide", [(d, (d + step) % wide) for d in places])

    every, first, second = range(wide), range(0, wide, 2), range(1, wide, 2)

    def swap(value):
        return lax.ppermute(value, "wide", [(d, d ^ 1) for d in every])

    near = [(send(v, -2, every), send(v, 2, every)) for v in own]
    far = [(send(after, -2, every), send(before, 1, second)) for after, before in near]
    streams = []
    for n, (v, (after, before)) in enumerate(zip(own, near)):
        if n == 0:
            before, coeffs = lax.optimization_barrier((before, coeffs))
        shared = [swap(v), swap(after), swap(before)]
        last, early = far[n]
        streams.append([v, after, before, last] + shared + [early, send(last, 1, first)])
    return streams, coeffs


def shards(voltages, station_flags, channel_order, beam_stations, beam_weight_re, beam_weight_im):
    _, width, _, length = voltages.shape
    wide, narrow = lax.axis_size("wide"), lax.axis_size("narrow")
    coeffs = held_coefficients(length, wide)
    own = [voltages[part, :, 0, :] for part in range(2)]
    streams, coeffs = gather_frames(own, coeffs, wide)
    own_flags = lax.dynamic_slice_in_dim(
        station_flags, lax.axis_index("narrow") * (width // 2), width // 2
    )
    gain = jnp.tile(jnp.repeat(own_flags, 2).astype(jnp.float32), 2)[None, :]
    index = channel_order % OUTER * LANES + channel_order // OUTER
    spectra = channelize(streams[0], streams[1], coeffs, index, gain)
    turned_over = lax.all_to_all(spectra, ("wide", "narrow"), 0, 0, tiled=True)
    voices = turned_over.reshape(wide, narrow, AVG, 2 * width)
    weights = beam_weights(beam_stations, beam_weight_re, beam_weight_im, width * narrow)
    sent = correlate(voices, weights)
    back = lax.all_to_all(sent, "narrow", 0, 0, tiled=True)
    visibilities = back[:, : 2 * width].astype(jnp.float32).reshape(narrow, 2, width, -1)
    beams = beam_stations.shape[0]
    terms = back[:, 2 * width :].astype(jnp.float32).reshape(narrow * AVG, -1)
    energy = terms[:, :beams] + terms[:, beams : 2 * beams] + terms[:, 2 * beams : 3 * beams]
    share = beams // narrow
    beam_power = lax.dynamic_slice_in_dim(energy, lax.axis_index("narrow") * share, share, axis=1)
    return (visibilities, beam_power)


def solution(mesh):
    return jax.shard_map(
        shards,
        mesh=mesh,
        in_specs=(P(None, "narrow", "wide", None), P(), P(), P(), P(), P()),
        out_specs=(P("wide", None, "narrow", None), P("wide", "narrow")),
        check_vma=False,
    )
```

```python
import math

import jax
import jax.numpy as jnp
import numpy as np
from jax import lax
from jax.experimental import pallas as pl
from jax.experimental.pallas import tpu as pltpu
from jax.sharding import PartitionSpec as P


TAPS = 8
AVG = 8
LANES = 128
OUTER = 32
ROWS = 16


LEAD = 4
TAPS_FIRST = (4, 2, 6, 0, 3, 1, 5, 7, TAPS)
TAPS_SECOND = (4, 2, 6, 0, 5, 3, 7, TAPS, 1)
HELD = len(TAPS_FIRST)


def prototype(tap_count, length):
    places = jnp.arange(tap_count * length, dtype=jnp.float32)
    offsets = places / length - tap_count / 2.0
    window = 0.5 - 0.5 * jnp.cos(2.0 * jnp.pi * (places + 0.5) / (tap_count * length))
    return (jnp.sinc(offsets) * window).reshape(tap_count, length)


def fourier_tables():
    length = OUTER * LANES
    inner = np.arange(LANES, dtype=np.float64)
    angle = 2.0 * np.pi * np.arange(OUTER, dtype=np.float64)[:, None] * inner[None, :] / length
    twist = np.stack([np.cos(angle), -np.sin(angle)]).astype(np.float32)
    turn = 2.0 * np.pi * ((np.arange(LANES)[:, None] * np.arange(LANES)[None, :]) % LANES) / LANES
    cos, sin = np.cos(turn), np.sin(turn)
    matrix = (np.block([[cos, -sin], [sin, cos]]) / math.sqrt(length)).astype(np.float32)
    high = matrix.astype(jnp.bfloat16)
    low = (matrix - high.astype(np.float32)).astype(jnp.bfloat16)
    return twist, high, low


def add(a, b):
    return (a[0] + b[0], a[1] + b[1])


def sub(a, b):
    return (a[0] - b[0], a[1] - b[1])


def turned(a, num, den):
    num %= den
    if num == 0:
        return a
    if 4 * num == den:
        return (a[1], -a[0])
    if 2 * num == den:
        return (-a[0], -a[1])
    if 4 * num == 3 * den:
        return (-a[1], a[0])
    cos, sin = math.cos(2.0 * math.pi * num / den), math.sin(2.0 * math.pi * num / den)
    return (a[0] * cos + a[1] * sin, a[1] * cos - a[0] * sin)


def four(x):
    s0, s1, s2, s3 = add(x[0], x[2]), sub(x[0], x[2]), add(x[1], x[3]), sub(x[1], x[3])
    r3 = turned(s3, 1, 4)
    return [add(s0, s2), add(s1, r3), sub(s0, s2), sub(s1, r3)]


def eight(x):
    even, odd = four(x[0::2]), four(x[1::2])
    odd = [turned(odd[q], q, 8) for q in range(4)]
    return [add(even[q], odd[q]) for q in range(4)] + [sub(even[q], odd[q]) for q in range(4)]


def channelize_kernel(index, *refs):
    frames_re, frames_im = refs[:HELD], refs[HELD : 2 * HELD]
    coeffs, twist, high, low, gain, out, mid, y_hi, y_lo, spec, lined, picked = refs[2 * HELD :]
    step = pl.program_id(0)

    def filtered(frames, block):
        span = slice(block * LANES, (block + 1) * LANES)
        total = coeffs[0:1, span] * frames[0][:, span].astype(jnp.float32)
        for tap in range(1, HELD):
            total = total + coeffs[tap : tap + 1, span] * frames[tap][:, span].astype(jnp.float32)
        return total

    for j in range(8):
        points = [
            (filtered(frames_re, j + 8 * m), filtered(frames_im, j + 8 * m)) for m in range(4)
        ]
        for p, value in enumerate(four(points)):
            value = turned(value, j * p, OUTER)
            mid[p, j, 0] = value[0]
            mid[p, j, 1] = value[1]
    for p in range(4):
        for q, value in enumerate(eight([(mid[p, j, 0], mid[p, j, 1]) for j in range(8)])):
            c = p + 4 * q
            cos, sin = twist[0, c : c + 1, :], twist[1, c : c + 1, :]
            rows = slice(c * ROWS, (c + 1) * ROWS)
            for part, y in enumerate(
                (value[0] * cos - value[1] * sin, value[0] * sin + value[1] * cos)
            ):
                upper = y.astype(jnp.bfloat16)
                lanes = slice(part * LANES, (part + 1) * LANES)
                y_hi[rows, lanes] = upper
                y_lo[rows, lanes] = (y - upper.astype(jnp.float32)).astype(jnp.bfloat16)

    def dot(a, b):
        return jnp.dot(a[...], b[...], preferred_element_type=jnp.float32)

    result = dot(y_hi, high) + (dot(y_lo, high) + dot(y_hi, low))
    start = pl.multiple_of(step * ROWS, ROWS)
    for part in range(2):
        spec[:, part, pl.ds(start, ROWS), :] = result[:, part * LANES : (part + 1) * LANES].reshape(
            OUTER, ROWS, LANES
        )

    @pl.when(step == pl.num_programs(0) - 1)
    def _():
        width = spec.shape[2]

        def line(c, carry):
            block = spec[c].reshape(2 * width, LANES)
            rows = pl.ds(pl.multiple_of(c * LANES, LANES), LANES)
            lined[rows, :] = block.astype(jnp.bfloat16).T.astype(jnp.float32) * gain[...]
            return carry

        lax.fori_loop(0, OUTER, line, 0, unroll=4)
        batch = 64

        def pick(g, carry):
            base = pl.multiple_of(g * batch, batch)
            for j in range(batch):
                picked[pl.ds(base + j, 1), :] = lined[pl.ds(index[base + j], 1), :]
            return carry

        lax.fori_loop(0, OUTER * LANES // batch, pick, 0)
        out[...] = picked[...].reshape(out.shape).astype(jnp.bfloat16)


def channelize(frames_re, frames_im, coeffs, index, gain):
    width, length = frames_re[0].shape
    twist, high, low = fourier_tables()
    frame = pl.BlockSpec((ROWS, length), lambda i, idx: (i, 0))

    def whole(shape):
        return pl.BlockSpec(shape, lambda i, idx: (0,) * len(shape))

    return pl.pallas_call(
        channelize_kernel,
        out_shape=jax.ShapeDtypeStruct((length // AVG, AVG, 2 * width), jnp.bfloat16),
        grid_spec=pltpu.PrefetchScalarGridSpec(
            num_scalar_prefetch=1,
            grid=(width // ROWS,),
            in_specs=[frame] * (2 * HELD)
            + [whole(coeffs.shape), whole(twist.shape), whole(high.shape), whole(low.shape)]
            + [whole(gain.shape)],
            out_specs=whole((length // AVG, AVG, 2 * width)),
            scratch_shapes=[
                pltpu.VMEM((4, 8, 2, ROWS, LANES), jnp.float32),
                pltpu.VMEM((OUTER * ROWS, 2 * LANES), jnp.bfloat16),
                pltpu.VMEM((OUTER * ROWS, 2 * LANES), jnp.bfloat16),
                pltpu.VMEM((OUTER, 2, width, LANES), jnp.float32),
                pltpu.VMEM((length, 2 * width), jnp.float32),
                pltpu.VMEM((length, 2 * width), jnp.float32),
            ],
        ),
        compiler_params=pltpu.CompilerParams(dimension_semantics=("arbitrary",)),
        name="channelize",
    )(index, *frames_re, *frames_im, coeffs, jnp.asarray(twist), jnp.asarray(high), jnp.asarray(low), gain)


def weights_kernel(stations, weight_re, weight_im, out):
    inputs = out.shape[0] // 2
    beams = stations.shape[1]
    chunk = 64

    def block(n, carry):
        start = pl.multiple_of(n * chunk, chunk)
        rows = lax.broadcasted_iota(jnp.int32, (chunk, beams), 0) + start
        station = rows // 2

        def pick(t, sums):
            here = stations[pl.ds(t, 1), :] == station
            return (
                sums[0] + jnp.where(here, weight_re[pl.ds(t, 1), :], 0.0),
                sums[1] + jnp.where(here, weight_im[pl.ds(t, 1), :], 0.0),
            )

        zero = jnp.zeros((chunk, beams), jnp.float32)
        sum_re, sum_im = lax.fori_loop(0, stations.shape[0], pick, (zero, zero), unroll=4)
        for pol in range(2):
            own = rows % 2 == pol
            part_re = jnp.where(own, sum_re, 0.0).astype(jnp.bfloat16)
            part_im = jnp.where(own, sum_im, 0.0).astype(jnp.bfloat16)
            first = slice(2 * pol * beams, (2 * pol + 1) * beams)
            second = slice((2 * pol + 1) * beams, (2 * pol + 2) * beams)
            out[pl.ds(start, chunk), first] = part_re
            out[pl.ds(start, chunk), second] = part_im
            out[pl.ds(inputs + start, chunk), first] = -part_im
            out[pl.ds(inputs + start, chunk), second] = part_re
        return carry

    lax.fori_loop(0, inputs // chunk, block, 0)


def beam_weights(beam_stations, weight_re, weight_im, input_count):
    beams = beam_stations.shape[0]
    return pl.pallas_call(
        weights_kernel,
        out_shape=jax.ShapeDtypeStruct((2 * input_count, 4 * beams), jnp.bfloat16),
        name="beam_weights",
    )(beam_stations.T, weight_re.T, weight_im.T)


def correlate_kernel(voices, weights, out, x_ref, xt_ref):
    frames, groups, avg, width = voices.shape
    half = width // 2
    count = groups * half
    depth = frames * avg
    lane = lax.broadcasted_iota(jnp.int32, (depth, width), 1)
    for m in range(groups // 2):
        a = voices[:, 2 * m].astype(jnp.float32).reshape(depth, width)
        b = voices[:, 2 * m + 1].astype(jnp.float32).reshape(depth, width)
        re = jnp.where(lane < half, a, pltpu.roll(b, half, 1))
        im = jnp.where(lane < half, pltpu.roll(a, half, 1), b)
        for part, value in enumerate((re, im)):
            span = slice(part * count + m * width, part * count + (m + 1) * width)
            x_ref[:, span] = value.astype(jnp.bfloat16)
            xt_ref[span, :] = value.T.astype(jnp.bfloat16)

    def dot(a, b):
        return jnp.dot(a, b, preferred_element_type=jnp.float32)

    power = dot(x_ref[...], weights[...])
    power = power * power
    beams = power.shape[1] // 4
    energy = power[:, :beams] + power[:, beams : 2 * beams]
    energy = energy + (power[:, 2 * beams : 3 * beams] + power[:, 3 * beams :])
    energy = jnp.sum(energy.reshape(frames, avg, beams), axis=0) / frames
    terms = []
    for _ in range(3):
        terms.append(energy.astype(jnp.bfloat16).astype(jnp.float32))
        energy = energy - terms[-1]
    share = beams // groups
    place = lax.broadcasted_iota(jnp.int32, (avg, beams), 1) // share

    scale = 1.0 / math.sqrt(depth)
    x_re, x_im = x_ref[:, :count], x_ref[:, count:]
    columns = count // LANES
    for r in range(groups):
        xt_re = xt_ref[r * half : (r + 1) * half, :]
        xt_im = xt_ref[count + r * half : count + (r + 1) * half, :]
        rows_re = (dot(xt_re, x_re) + dot(xt_im, x_im)) * scale
        rows_im = (dot(xt_im, x_re) - dot(xt_re, x_im)) * scale
        for part, rows in enumerate((rows_re, rows_im)):
            for c in range(columns):
                tiles = rows[:, c * LANES : (c + 1) * LANES].reshape(half // avg, avg, LANES)
                start = (part * columns + c) * (half // avg)
                out[r, start : start + half // avg] = tiles.astype(jnp.bfloat16)
        packed = jnp.zeros_like(energy)
        for n, term in enumerate(terms):
            shift = (n - r) * share % beams
            moved = pltpu.roll(term, shift, 1) if shift else term
            packed = jnp.where(place == n, moved, packed)
        out[r, out.shape[1] - 1] = packed.astype(jnp.bfloat16)


def correlate(voices, weights):
    frames, groups, avg, width = voices.shape
    count = groups * width // 2
    depth = frames * avg
    return pl.pallas_call(
        correlate_kernel,
        out_shape=jax.ShapeDtypeStruct(
            (groups, width * count // (avg * LANES) + 1, avg, LANES), jnp.bfloat16
        ),
        in_specs=[
            pl.BlockSpec(memory_space=pltpu.VMEM),
            pl.BlockSpec(memory_space=pltpu.VMEM),
        ],
        scratch_shapes=[
            pltpu.VMEM((depth, 2 * count), jnp.bfloat16),
            pltpu.VMEM((2 * count, depth), jnp.bfloat16),
        ],
        name="correlate",
    )(voices, weights)


def unpack(tiles, half, count, share):
    groups, _, avg, _ = tiles.shape
    rows = tiles[:, :-1].astype(jnp.float32).reshape(groups, 2, count // LANES, half // avg, avg, LANES)
    rows = rows.transpose(0, 1, 3, 4, 2, 5).reshape(groups, 2, half, count)
    terms = tiles[:, -1].astype(jnp.float32).reshape(groups * avg, LANES)
    power = terms[:, :share] + terms[:, share : 2 * share] + terms[:, 2 * share : 3 * share]
    return (rows, power)


def held_coefficients(length, wide):
    place = lax.axis_index("wide")
    frame = (place + LEAD) % wide
    taps = jnp.where(place % 2 == 0, jnp.array(TAPS_FIRST), jnp.array(TAPS_SECOND))
    picked = taps[:, None] == jnp.arange(TAPS)[None, :]
    used = jnp.logical_and(picked, (taps <= frame)[:, None])
    table = prototype(TAPS, length)
    rows = [jnp.where(used[:, tap, None], table[tap], 0.0) for tap in range(TAPS)]
    return sum(rows[1:], rows[0])


def gather_frames(own, coeffs, wide):
    def send(value, step, places):
        return lax.ppermute(value, "wide", [(d, (d + step) % wide) for d in places])

    every, first, second = range(wide), range(0, wide, 2), range(1, wide, 2)

    def swap(value):
        return lax.ppermute(value, "wide", [(d, d ^ 1) for d in every])

    near = [(send(v, -2, every), send(v, 2, every)) for v in own]
    far = [(send(after, -2, every), send(before, 1, second)) for after, before in near]
    streams = []
    for n, (v, (after, before)) in enumerate(zip(own, near)):
        if n == 0:
            before, coeffs = lax.optimization_barrier((before, coeffs))
        shared = [swap(v), swap(after), swap(before)]
        last, early = far[n]
        streams.append([v, after, before, last] + shared + [early, send(last, 1, first)])
    return streams, coeffs


def shards(voltages, station_flags, channel_order, beam_stations, beam_weight_re, beam_weight_im):
    _, width, _, length = voltages.shape
    wide, narrow = lax.axis_size("wide"), lax.axis_size("narrow")
    own_flags = lax.dynamic_slice_in_dim(
        station_flags, lax.axis_index("narrow") * (width // 2), width // 2
    )
    gain = jnp.tile(jnp.repeat(own_flags, 2).astype(jnp.float32), 2)[None, :]
    index = channel_order % OUTER * LANES + channel_order // OUTER
    beside = (held_coefficients(length, wide), index, gain)
    own = [voltages[part, :, 0, :] for part in range(2)]
    streams, (coeffs, index, gain) = gather_frames(own, beside, wide)
    spectra = channelize(streams[0], streams[1], coeffs, index, gain)
    turned_over = lax.all_to_all(spectra, ("wide", "narrow"), 0, 0, tiled=True)
    voices = turned_over.reshape(wide, narrow, AVG, 2 * width)
    weights = beam_weights(beam_stations, beam_weight_re, beam_weight_im, width * narrow)
    voices = pltpu.with_memory_space_constraint(voices, pltpu.VMEM)
    sent = correlate(voices, weights)
    back = lax.all_to_all(sent, "narrow", 0, 0, tiled=True)
    share = beam_stations.shape[0] // narrow
    return unpack(back, width, width * narrow, share)


def solution(mesh):
    return jax.shard_map(
        shards,
        mesh=mesh,
        in_specs=(P(None, "narrow", "wide", None), P(), P(), P(), P(), P()),
        out_specs=(P("wide", None, "narrow", None), P("wide", "narrow")),
        check_vma=False,
    )
```
